32 devices in a mesh: shard: 2 (over x), ctx: 4 (over y, core), tp: 4 (over z).
Axes of the slice: x: 2, y: 2, z: 4, core: 2. Of those that a mesh axis runs over, the one named last changes fastest.
Arguments:
- hidden_in: bfloat16 [4, 1024, 1024], P('shard', 'ctx'), may hold values from -6 to 6
- lengths: int32 [4], P('shard'), may hold values from 1 to 1024, as said below
- cotangent: bfloat16 [4, 1024, 1024], P('shard', 'ctx'), may hold values from -6 to 6
- ln1_gain: bfloat16 [1024], P(('shard', 'ctx')), may hold values from 0.5 to 1.5
- ln1_bias: bfloat16 [1024], P(('shard', 'ctx')), may hold values from -3 to 3
- w_qkv: bfloat16 [3, 1024, 1024], P(None, ('shard', 'ctx'), 'tp'), may hold values from -0.1875 to 0.1875
- b_qv: bfloat16 [2, 1024], P(None, 'tp'), may hold values from -3 to 3
- w_out: bfloat16 [1024, 1024], P(('shard', 'ctx'), 'tp'), may hold values from -1.5 to 1.5
- b_out: bfloat16 [1024], P(('shard', 'ctx')), may hold values from -3 to 3
- ln2_gain: bfloat16 [1024], P(('shard', 'ctx')), may hold values from 0.5 to 1.5
- ln2_bias: bfloat16 [1024], P(('shard', 'ctx')), may hold values from -3 to 3
- w_up: bfloat16 [1024, 4096], P(('shard', 'ctx'), 'tp'), may hold values from -0.1875 to 0.1875
- b_up: bfloat16 [4096], P('tp'), may hold values from -3 to 3
- w_down: bfloat16 [1024, 4096], P(('shard', 'ctx'), 'tp'), may hold values from -0.375 to 0.375
- b_down: bfloat16 [1024], P(('shard', 'ctx')), may hold values from -3 to 3
Outputs:
- hidden_out: float32 [4, 1024, 1024], P('shard', 'ctx')
- grad_in: float32 [4, 1024, 1024], P('shard', 'ctx')
- grad_ln1_gain: float32 [1024], P(('shard', 'ctx'))
- grad_ln1_bias: float32 [1024], P(('shard', 'ctx'))
- grad_w_qkv: float32 [3, 1024, 1024], P(None, ('shard', 'ctx'), 'tp')
- grad_b_qv: float32 [2, 1024], P(None, 'tp')
- grad_w_out: float32 [1024, 1024], P(('shard', 'ctx'), 'tp')
- grad_b_out: float32 [1024], P(('shard', 'ctx'))
- grad_ln2_gain: float32 [1024], P(('shard', 'ctx'))
- grad_ln2_bias: float32 [1024], P(('shard', 'ctx'))
- grad_w_up: float32 [1024, 4096], P(('shard', 'ctx'), 'tp')
- grad_b_up: float32 [4096], P('tp')
- grad_w_down: float32 [1024, 4096], P(('shard', 'ctx'), 'tp')
- grad_b_down: float32 [1024], P(('shard', 'ctx'))
The draws below stay inside these ranges and needn't reach their ends.
Inputs may be any that keep to these rules, and one draw needn't show every extreme that they name: Sequence i belongs to shard group i // 2; its positions from lengths[i] on are padding. Some sequence has all 1024 positions live.
All inputs are finite; a program needn't handle non-finite values.
Results may differ from the reference program's by a relative error of at most 0.012.
The reference program's roundings to bfloat16 on the way count: a program that leaves them out, or rounds other values in their place, can miss the bound.
Values may be sent and summed in bfloat16 or wider, within the bound.
A program may use at most 128 MiB of HBM per device.

```python
import math
import jax
import jax.numpy as jnp
from jax import lax

D = 1024
HEADS = 16
HD = 64
FF = 4096
SEQ = 1024
SEQS_GRP = 2
NSEQ = 4


def draw_lengths(key, part):
    groups = NSEQ // SEQS_GRP
    key_base, key_scale, key_full = jax.random.split(key, 3)
    base = jax.random.randint(key_base, (NSEQ,), SEQ // 4, SEQ + 1)
    factor = jax.random.randint(key_scale, (groups,), 1, 5)
    spread = jnp.repeat(factor, SEQS_GRP, total_repeat_length=NSEQ)
    drawn = jnp.maximum(base * spread // 4, 1)
    chosen = jax.random.randint(key_full, (), 0, NSEQ)
    drawn = jnp.where(jnp.arange(NSEQ) == chosen, SEQ, drawn)
    return drawn.astype(jnp.int32)


def steps_of(own_key, dims, cuts, low, high):
    factor_of, own = 1.0, jax.random.fold_in(own_key, 6)
    for position, blocks in cuts:
        draws = jnp.exp(jax.random.uniform(jax.random.fold_in(own, position), (blocks,), jnp.float32, low / len(cuts), high / len(cuts)))
        factor_of = factor_of * jnp.repeat(draws, dims[position] // blocks).reshape([-1 if axis == position else 1 for axis in range(len(dims))])
    return factor_of


def gaussian(rng, shape, width, limit, pieces=(), kind=jnp.bfloat16):
    array = jax.random.normal(rng, shape, jnp.float32) * width
    if len(pieces) > 0:
        array = steps_of(rng, shape, pieces, -0.22, 0.18) * array
    return jnp.clip(array, min=-limit, max=limit).astype(kind)


def setup_inputs(seed: int = 0) -> dict:
    key_of = jax.random.split(jax.random.key(seed), 16)
    hidden_in = gaussian(key_of[0], (NSEQ, SEQ, D), 1.0, 6.0, ((0, 2), (1, 4)))
    lengths = draw_lengths(jax.random.fold_in(key_of[15], 71), 0)
    cotangent = gaussian(key_of[2], (NSEQ, SEQ, D), 1.0, 6.0, ((0, 2), (1, 4)))
    ln1_gain = jnp.clip(1.0 + 0.1 * jax.random.normal(key_of[3], (D,), jnp.float32), 0.5, 1.5).astype(jnp.bfloat16)
    ln1_bias = gaussian(key_of[4], (D,), 0.5, 3.0, ((0, 8),))
    w_qkv = gaussian(key_of[5], (3, D, D), D ** -0.5, 0.1875, ((1, 8), (2, 4)))
    b_qv = gaussian(key_of[6], (2, D), 0.5, 3.0, ((1, 4),))
    w_out = gaussian(key_of[7], (D, D), (D // 64) ** -0.5, 1.5, ((0, 8), (1, 4)))
    b_out = gaussian(key_of[8], (D,), 0.5, 3.0, ((0, 8),))
    ln2_gain = jnp.clip(1.0 + 0.1 * jax.random.normal(key_of[9], (D,), jnp.float32), 0.5, 1.5).astype(jnp.bfloat16)
    ln2_bias = gaussian(key_of[10], (D,), 0.5, 3.0, ((0, 8),))
    w_up = gaussian(key_of[11], (D, FF), D ** -0.5, 0.1875, ((0, 8), (1, 4)))
    b_up = gaussian(key_of[12], (FF,), 0.5, 3.0, ((0, 4),))
    w_down = gaussian(key_of[13], (D, FF), (FF // 16) ** -0.5, 0.375, ((0, 8), (1, 4)))
    b_down = gaussian(key_of[14], (D,), 0.5, 3.0, ((0, 8),))
    return {"hidden_in": hidden_in, "lengths": lengths, "cotangent": cotangent, "ln1_gain": ln1_gain, "ln1_bias": ln1_bias, "w_qkv": w_qkv, "b_qv": b_qv, "w_out": w_out, "b_out": b_out, "ln2_gain": ln2_gain, "ln2_bias": ln2_bias, "w_up": w_up, "b_up": b_up, "w_down": w_down, "b_down": b_down}


EPS = 1e-05
KAPPA = math.sqrt(2.0 / math.pi)

def normalize(row, gain, shift):
    center = lax.optimization_barrier(jnp.mean(row, axis=-1, keepdims=True))
    centred = row - center
    inv_std = lax.rsqrt(lax.optimization_barrier(jnp.mean(centred * centred, axis=-1, keepdims=True)) + EPS)
    unit_rows = centred * inv_std
    return (unit_rows * gain + shift, unit_rows, inv_std)

def normalize_back(grad_out, unit_rows, inv_std, gain):
    scaled = grad_out * gain
    return inv_std * (scaled - lax.optimization_barrier(jnp.mean(scaled, axis=-1, keepdims=True)) - unit_rows * lax.optimization_barrier(jnp.mean(scaled * unit_rows, axis=-1, keepdims=True)))

def gelu_pair(pre_act):
    inner = KAPPA * (pre_act + 0.044715 * pre_act * pre_act * pre_act)
    tanh_val = jnp.tanh(inner)
    value_out = 0.5 * pre_act * (1.0 + tanh_val)
    slope = 0.5 * (1.0 + tanh_val) + 0.5 * pre_act * (1.0 - tanh_val * tanh_val) * KAPPA * (1.0 + 3.0 * 0.044715 * pre_act * pre_act)
    return (value_out, slope)

def rounded(value_in):
    return lax.optimization_barrier(value_in.astype(jnp.bfloat16)).astype(jnp.float32)

def reference(hidden_in, lengths, cotangent, ln1_gain, ln1_bias, w_qkv, b_qv, w_out, b_out, ln2_gain, ln2_bias, w_up, b_up, w_down, b_down):
    gain_one = ln1_gain.astype(jnp.float32)
    shift_one = ln1_bias.astype(jnp.float32)
    gain_two = ln2_gain.astype(jnp.float32)
    shift_two = ln2_bias.astype(jnp.float32)
    bias_out = b_out.astype(jnp.float32)
    bias_down = b_down.astype(jnp.float32)
    bias_up = b_up.astype(jnp.float32)
    bias_query = b_qv[0].astype(jnp.float32)
    bias_value = b_qv[1].astype(jnp.float32)
    qkv_wide = w_qkv.astype(jnp.float32)
    scale = 1.0 / math.sqrt(HD)
    positions = jnp.arange(SEQ, dtype=jnp.int32)
    causal = positions[None, :] <= positions[:, None]

    def per_sequence(carry, item):
        rows_in, length, cotan = item
        live = (positions < length)[:, None]
        allowed = (causal & (positions[None, :] < length))[None]
        inputs = rows_in.astype(jnp.float32)
        normed_one, unit_one, inv_one = normalize(inputs, gain_one, shift_one)
        normed_bf = normed_one.astype(jnp.bfloat16)
        query = (jnp.dot(normed_bf, w_qkv[0], preferred_element_type=jnp.float32) + bias_query).astype(jnp.bfloat16)
        keys = jnp.dot(normed_bf, w_qkv[1], preferred_element_type=jnp.float32).astype(jnp.bfloat16)
        values = (jnp.dot(normed_bf, w_qkv[2], preferred_element_type=jnp.float32) + bias_value).astype(jnp.bfloat16)
        query_heads = query.astype(jnp.float32).reshape(SEQ, HEADS, HD)
        key_heads = keys.astype(jnp.float32).reshape(SEQ, HEADS, HD)
        value_heads = values.astype(jnp.float32).reshape(SEQ, HEADS, HD)
        scores = jnp.einsum('qhd,khd->hqk', query_heads, key_heads) * scale
        scores = jnp.where(allowed, scores, -1e+30)
        top = lax.optimization_barrier(jnp.max(scores, axis=-1, keepdims=True))
        log_total = top + jnp.log(lax.optimization_barrier(jnp.sum(jnp.exp(scores - top), axis=-1, keepdims=True)))
        exact_probs = jnp.where(allowed, jnp.exp(scores - log_total), 0.0)
        probs = rounded(exact_probs)
        attended = jnp.einsum('hqk,khd->qhd', probs, value_heads).reshape(SEQ, D).astype(jnp.bfloat16)
        resid = inputs + jnp.dot(attended, w_out.T, preferred_element_type=jnp.float32) + bias_out
        normed_two, unit_two, inv_two = normalize(resid, gain_two, shift_two)
        second_bf = normed_two.astype(jnp.bfloat16)
        pre_act = jnp.dot(second_bf, w_up, preferred_element_type=jnp.float32) + bias_up
        activ, slope = gelu_pair(pre_act)
        hidden = activ.astype(jnp.bfloat16)
        result = jnp.where(live, resid + jnp.dot(hidden, w_down.T, preferred_element_type=jnp.float32) + bias_down, 0.0)
        grad_rows = jnp.where(live, cotan.astype(jnp.float32), 0.0)
        grad_bf = grad_rows.astype(jnp.bfloat16)
        d_pre = jnp.dot(grad_bf, w_down, preferred_element_type=jnp.float32) * slope
        d_pre_bf = d_pre.astype(jnp.bfloat16)
        back_two = jnp.dot(d_pre_bf, w_up.T, preferred_element_type=jnp.float32)
        d_resid = grad_rows + normalize_back(back_two, unit_two, inv_two, gain_two)
        d_resid_bf = d_resid.astype(jnp.bfloat16)
        d_attended = jnp.dot(d_resid_bf, w_out, preferred_element_type=jnp.float32).astype(jnp.bfloat16)
        d_att_heads = d_attended.astype(jnp.float32).reshape(SEQ, HEADS, HD)
        att_heads = attended.astype(jnp.float32).reshape(SEQ, HEADS, HD)
        delta = jnp.transpose(lax.optimization_barrier(jnp.sum(d_att_heads * att_heads, axis=-1)))[:, :, None]
        d_probs = jnp.einsum('qhd,khd->hqk', d_att_heads, value_heads)
        d_scores = rounded(exact_probs * (d_probs - delta))
        d_query = (jnp.einsum('hqk,khd->qhd', d_scores, key_heads) * scale).reshape(SEQ, D)
        d_keys = (jnp.einsum('hqk,qhd->khd', d_scores, query_heads) * scale).reshape(SEQ, D)
        d_values = jnp.einsum('hqk,qhd->khd', probs, d_att_heads).reshape(SEQ, D)
        stacked = jnp.stack([d_query, d_keys, d_values], 0).astype(jnp.bfloat16)
        stacked_wide = stacked.astype(jnp.float32)
        back_one = jnp.einsum('jre,jde->rd', stacked_wide, qkv_wide)
        d_inputs = d_resid + normalize_back(back_one, unit_one, inv_one, gain_one)
        acc_gain_one, acc_shift_one, acc_qkv, acc_bias_qv, acc_out, acc_bias_out, acc_gain_two, acc_shift_two, acc_up, acc_bias_up, acc_down, acc_bias_down = carry
        carry = (acc_gain_one + lax.optimization_barrier(jnp.sum(back_one * unit_one, axis=0)), acc_shift_one + lax.optimization_barrier(jnp.sum(back_one, axis=0)), acc_qkv + jnp.einsum('rd,jre->jde', normed_bf.astype(jnp.float32), stacked_wide), acc_bias_qv + jnp.stack([lax.optimization_barrier(jnp.sum(d_query, axis=0)), lax.optimization_barrier(jnp.sum(d_values, axis=0))], 0), acc_out + jnp.dot(d_resid_bf.T, attended, preferred_element_type=jnp.float32), acc_bias_out + lax.optimization_barrier(jnp.sum(d_resid, axis=0)), acc_gain_two + lax.optimization_barrier(jnp.sum(back_two * unit_two, axis=0)), acc_shift_two + lax.optimization_barrier(jnp.sum(back_two, axis=0)), acc_up + jnp.dot(second_bf.T, d_pre_bf, preferred_element_type=jnp.float32), acc_bias_up + lax.optimization_barrier(jnp.sum(d_pre, axis=0)), acc_down + jnp.dot(grad_bf.T, hidden, preferred_element_type=jnp.float32), acc_bias_down + lax.optimization_barrier(jnp.sum(grad_rows, axis=0)))
        return (carry, (result, d_inputs))
    start = (jnp.zeros((D,), jnp.float32), jnp.zeros((D,), jnp.float32), jnp.zeros((3, D, D), jnp.float32), jnp.zeros((2, D), jnp.float32), jnp.zeros((D, D), jnp.float32), jnp.zeros((D,), jnp.float32), jnp.zeros((D,), jnp.float32), jnp.zeros((D,), jnp.float32), jnp.zeros((D, FF), jnp.float32), jnp.zeros((FF,), jnp.float32), jnp.zeros((D, FF), jnp.float32), jnp.zeros((D,), jnp.float32))
    final, (hidden_out, grad_in) = lax.scan(per_sequence, start, (hidden_in, lengths, cotangent))
    grad_ln1_gain, grad_ln1_bias, grad_w_qkv, grad_b_qv, grad_w_out, grad_b_out, grad_ln2_gain, grad_ln2_bias, grad_w_up, grad_b_up, grad_w_down, grad_b_down = final
    return (hidden_out, grad_in, grad_ln1_gain, grad_ln1_bias, grad_w_qkv, grad_b_qv, grad_w_out, grad_b_out, grad_ln2_gain, grad_ln2_bias, grad_w_up, grad_b_up, grad_w_down, grad_b_down)
```

```python
import math

import jax
import jax.numpy as jnp
from jax import lax
from jax.sharding import PartitionSpec as P

HD = 64


EPS = 1e-05
KAPPA = math.sqrt(2.0 / math.pi)


def normalize(row, gain, shift):
    center = jnp.mean(row, axis=-1, keepdims=True)
    centred = row - center
    inv_std = lax.rsqrt(jnp.mean(centred * centred, axis=-1, keepdims=True) + EPS)
    unit_rows = centred * inv_std
    return (unit_rows * gain + shift, unit_rows, inv_std)


def normalize_back(grad_out, unit_rows, inv_std, gain):
    scaled = grad_out * gain
    return inv_std * (
        scaled
        - jnp.mean(scaled, axis=-1, keepdims=True)
        - unit_rows * jnp.mean(scaled * unit_rows, axis=-1, keepdims=True)
    )


def gelu_pair(pre_act):
    inner = KAPPA * (pre_act + 0.044715 * pre_act * pre_act * pre_act)
    tanh_val = jnp.tanh(inner)
    value_out = 0.5 * pre_act * (1.0 + tanh_val)
    slope = 0.5 * (1.0 + tanh_val) + 0.5 * pre_act * (1.0 - tanh_val * tanh_val) * KAPPA * (
        1.0 + 3.0 * 0.044715 * pre_act * pre_act
    )
    return (value_out, slope)


def contract_last(left, right):
    return lax.dot_general(
        left, right, (((1,), (1,)), ((), ())), preferred_element_type=jnp.float32
    )


def contract_first(left, right):
    return lax.dot_general(
        left, right, (((0,), (0,)), ((), ())), preferred_element_type=jnp.float32
    )


def sum_tp(part):
    return lax.psum(part.astype(jnp.bfloat16), "tp").astype(jnp.float32)


def on_device(
    hidden_in,
    lengths,
    cotangent,
    ln1_gain,
    ln1_bias,
    w_qkv,
    b_qv,
    w_out,
    b_out,
    ln2_gain,
    ln2_bias,
    w_up,
    b_up,
    w_down,
    b_down,
):
    groups, block_len, width = hidden_in.shape
    head_width = w_qkv.shape[2]
    heads_here = head_width // HD
    row_count = groups * block_len
    scale = 1.0 / math.sqrt(HD)
    rows_own = w_out.shape[0]
    vectors = jnp.stack([ln1_gain, ln1_bias, b_out, ln2_gain, ln2_bias, b_down], 1)
    packed_one = jnp.concatenate(
        [w_qkv[0], w_qkv[1], w_qkv[2], w_out, jnp.pad(vectors, ((0, 0), (0, 122)))], 1
    )
    packed_two = jnp.concatenate([w_up, w_down], 1)
    whole_one = lax.all_gather(packed_one, ("shard", "ctx"), axis=0, tiled=True)
    whole_two = lax.all_gather(packed_two, ("shard", "ctx"), axis=0, tiled=True)
    qkv_width = 3 * head_width
    qkv_full = whole_one[:, :qkv_width]
    out_full = whole_one[:, qkv_width : qkv_width + head_width]
    vec_wide = whole_one[:, qkv_width + head_width :].astype(jnp.float32).T
    up_full = whole_two[:, : w_up.shape[1]]
    down_full = whole_two[:, w_up.shape[1] :]
    gain_one = vec_wide[0]
    shift_one = vec_wide[1]
    bias_out = vec_wide[2]
    gain_two = vec_wide[3]
    shift_two = vec_wide[4]
    bias_down = vec_wide[5]
    ctx_index = lax.axis_index("ctx")
    positions = jnp.arange(block_len, dtype=jnp.int32) + ctx_index * block_len
    live_rows = (positions[None, :] < lengths[:, None]).reshape(row_count, 1)

    def allowed_mask(start, count):
        key_pos = start + jnp.arange(count, dtype=jnp.int32)
        causal = key_pos[None, None, None, :] <= positions[None, None, :, None]
        inside = key_pos[None, None, None, :] < lengths[:, None, None, None]
        return causal & inside

    inputs = hidden_in.reshape(row_count, width).astype(jnp.float32)
    normed_one, unit_one, inv_one = normalize(inputs, gain_one, shift_one)
    normed_bf = normed_one.astype(jnp.bfloat16)
    product = jnp.dot(normed_bf, qkv_full, preferred_element_type=jnp.float32)
    projected = [product[:, j * head_width : (j + 1) * head_width] for j in range(3)]
    query = (projected[0] + b_qv[0].astype(jnp.float32)).astype(jnp.bfloat16)
    keys_here = projected[1].astype(jnp.bfloat16).reshape(groups, block_len, head_width)
    values_here = (
        (projected[2] + b_qv[1].astype(jnp.float32))
        .astype(jnp.bfloat16)
        .reshape(groups, block_len, head_width)
    )
    query_heads = query.reshape(groups, block_len, heads_here, HD)

    kv_whole = lax.all_gather(
        jnp.concatenate([keys_here, values_here], -1), "ctx", axis=1, tiled=True
    )
    keys_whole, values_whole = kv_whole[..., :head_width], kv_whole[..., head_width:]

    def fold_keys(step_fn, init):
        return step_fn(init, (keys_whole, values_whole), jnp.int32(0))

    def piece_scores(piece, start):
        key_piece, value_piece = piece
        count = key_piece.shape[1]
        key_heads = key_piece.reshape(groups, count, heads_here, HD)
        value_heads = value_piece.reshape(groups, count, heads_here, HD)
        scores = (
            jnp.einsum(
                "sqhd,skhd->shqk", query_heads, key_heads, preferred_element_type=jnp.float32
            )
            * scale
        )
        allowed = allowed_mask(start, count)
        return (jnp.where(allowed, scores, -1e30), allowed, value_heads)

    def totals_step(carry, piece, start):
        top, total = carry
        scores, allowed, unused = piece_scores(piece, start)
        new_top = jnp.maximum(top, jnp.max(scores, axis=-1))
        weights = jnp.where(allowed, jnp.exp(scores - new_top[..., None]), 0.0)
        total = jnp.sum(weights, axis=-1)
        return (new_top, total)

    start_totals = (
        jnp.full((groups, heads_here, block_len), -1e30, jnp.float32),
        jnp.zeros((groups, heads_here, block_len), jnp.float32),
    )
    top, total = fold_keys(totals_step, start_totals)
    log_total = top + jnp.log(total)

    def values_step(accum, piece, start):
        scores, allowed, value_heads = piece_scores(piece, start)
        probs_piece = jnp.where(allowed, jnp.exp(scores - log_total[..., None]), 0.0).astype(
            jnp.bfloat16
        )
        return jnp.einsum(
            "shqk,skhd->sqhd", probs_piece, value_heads, preferred_element_type=jnp.float32
        )

    accum = fold_keys(values_step, jnp.zeros((groups, block_len, heads_here, HD), jnp.float32))
    attended_heads = accum.astype(jnp.bfloat16)
    attended = attended_heads.reshape(row_count, head_width)
    proj_sum = sum_tp(contract_last(attended, out_full))
    resid = inputs + proj_sum + bias_out
    normed_two, unit_two, inv_two = normalize(resid, gain_two, shift_two)
    second_bf = normed_two.astype(jnp.bfloat16)
    pre_act = jnp.dot(second_bf, up_full, preferred_element_type=jnp.float32) + b_up.astype(
        jnp.float32
    )
    activ, slope = gelu_pair(pre_act)
    hidden = activ.astype(jnp.bfloat16)
    mlp_sum = sum_tp(contract_last(hidden, down_full))
    result = jnp.where(live_rows, resid + mlp_sum + bias_down, 0.0)
    grad_rows = jnp.where(live_rows, cotangent.reshape(row_count, width).astype(jnp.float32), 0.0)
    grad_bf = grad_rows.astype(jnp.bfloat16)
    grad_bias_down = jnp.sum(grad_rows, axis=0)
    grad_down = contract_first(grad_bf, hidden)
    d_pre = jnp.dot(grad_bf, down_full, preferred_element_type=jnp.float32) * slope
    d_pre_bf = d_pre.astype(jnp.bfloat16)
    grad_bias_up = jnp.sum(d_pre, axis=0)
    grad_up = contract_first(second_bf, d_pre_bf)
    back_two = sum_tp(contract_last(d_pre_bf, up_full))
    grad_gain_two = jnp.sum(back_two * unit_two, axis=0)
    grad_shift_two = jnp.sum(back_two, axis=0)
    d_resid = grad_rows + normalize_back(back_two, unit_two, inv_two, gain_two)
    d_resid_bf = d_resid.astype(jnp.bfloat16)
    grad_bias_out = jnp.sum(d_resid, axis=0)
    grad_out = contract_first(d_resid_bf, attended)
    d_attended = jnp.dot(d_resid_bf, out_full, preferred_element_type=jnp.float32).astype(
        jnp.bfloat16
    )
    seq_len = keys_whole.shape[1]
    key_heads = keys_whole.reshape(groups, seq_len, heads_here, HD)
    value_heads = values_whole.reshape(groups, seq_len, heads_here, HD)
    scores = (
        jnp.einsum("sqhd,skhd->shqk", query_heads, key_heads, preferred_element_type=jnp.float32)
        * scale
    )
    allowed = allowed_mask(0, seq_len)
    exact_probs = jnp.where(allowed, jnp.exp(scores - log_total[..., None]), 0.0)
    d_att_heads = d_attended.reshape(groups, block_len, heads_here, HD)
    delta = jnp.transpose(
        jnp.sum(d_att_heads.astype(jnp.float32) * attended_heads.astype(jnp.float32), axis=-1),
        (0, 2, 1),
    )
    d_probs = jnp.einsum(
        "sqhd,skhd->shqk", d_att_heads, value_heads, preferred_element_type=jnp.float32
    )
    d_scores = (exact_probs * (d_probs - delta[..., None])).astype(jnp.bfloat16)
    d_query = (
        jnp.einsum("shqk,skhd->sqhd", d_scores, key_heads, preferred_element_type=jnp.float32)
        * scale
    )
    probs_bf = exact_probs.astype(jnp.bfloat16)
    key_terms = (
        jnp.einsum("shqk,sqhd->skhd", d_scores, query_heads, preferred_element_type=jnp.float32)
        * scale
    )
    value_terms = jnp.einsum(
        "shqk,sqhd->skhd", probs_bf, d_att_heads, preferred_element_type=jnp.float32
    )
    kv_terms = jnp.concatenate(
        [
            key_terms.reshape(groups, seq_len, head_width).astype(jnp.bfloat16),
            value_terms.reshape(groups, seq_len, head_width).astype(jnp.bfloat16),
        ],
        -1,
    )
    kv_sum = lax.psum_scatter(kv_terms, "ctx", scatter_dimension=1, tiled=True).astype(jnp.float32)
    d_keys, d_values = kv_sum[..., :head_width], kv_sum[..., head_width:]
    d_query_rows = d_query.reshape(row_count, head_width)
    d_value_rows = d_values.reshape(row_count, head_width)
    grad_bias_qv = jnp.stack([jnp.sum(d_query_rows, axis=0), jnp.sum(d_value_rows, axis=0)], 0)
    stacked = jnp.concatenate(
        [d_query_rows, d_keys.reshape(row_count, head_width), d_value_rows], 1
    ).astype(jnp.bfloat16)
    grad_qkv = contract_first(normed_bf, stacked)
    back_one = sum_tp(contract_last(stacked, qkv_full))
    grad_gain_one = jnp.sum(back_one * unit_one, axis=0)
    grad_shift_one = jnp.sum(back_one, axis=0)
    d_inputs = d_resid + normalize_back(back_one, unit_one, inv_one, gain_one)
    vec_grads = jnp.concatenate(
        [
            grad_gain_one,
            grad_shift_one,
            grad_bias_out,
            grad_gain_two,
            grad_shift_two,
            grad_bias_down,
            grad_bias_qv.reshape(-1),
            grad_bias_up,
        ]
    )
    back_pair = jnp.concatenate([grad_qkv, grad_out], 1).astype(jnp.bfloat16)
    ffn_pair = jnp.concatenate([grad_up, grad_down], 1).astype(jnp.bfloat16)
    sum_ffn = lax.psum_scatter(
        ffn_pair, ("shard", "ctx"), scatter_dimension=0, tiled=True
    ).astype(jnp.float32)
    sum_back = lax.psum_scatter(
        back_pair, ("shard", "ctx"), scatter_dimension=0, tiled=True
    ).astype(jnp.float32)
    sum_qkv = jnp.stack(
        [sum_back[:, j * head_width : (j + 1) * head_width] for j in range(3)], 0
    )
    sum_out = sum_back[:, qkv_width:]
    sum_up, sum_down = sum_ffn[:, : w_up.shape[1]], sum_ffn[:, w_up.shape[1] :]
    all_vec = lax.psum(vec_grads, ("shard", "ctx"))
    own = lax.axis_index(("shard", "ctx")) * rows_own
    sum_vec = lax.dynamic_slice(all_vec[: 6 * width].reshape(6, width), (0, own), (6, rows_own))
    bias_qv_sum = all_vec[6 * width : 6 * width + 2 * head_width].reshape(2, head_width)
    bias_up_sum = all_vec[6 * width + 2 * head_width :]
    return (
        result.reshape(groups, block_len, width),
        d_inputs.reshape(groups, block_len, width),
        sum_vec[0],
        sum_vec[1],
        sum_qkv,
        bias_qv_sum,
        sum_out,
        sum_vec[2],
        sum_vec[3],
        sum_vec[4],
        sum_up,
        bias_up_sum,
        sum_down,
        sum_vec[5],
    )


def solution(mesh):
    return jax.shard_map(
        on_device,
        mesh=mesh,
        in_specs=(
            P("shard", "ctx", None),
            P("shard"),
            P("shard", "ctx", None),
            P(("shard", "ctx")),
            P(("shard", "ctx")),
            P(None, ("shard", "ctx"), "tp"),
            P(None, "tp"),
            P(("shard", "ctx"), "tp"),
            P(("shard", "ctx")),
            P(("shard", "ctx")),
            P(("shard", "ctx")),
            P(("shard", "ctx"), "tp"),
            P("tp"),
            P(("shard", "ctx"), "tp"),
            P(("shard", "ctx")),
        ),
        out_specs=(
            P("shard", "ctx", None),
            P("shard", "ctx", None),
            P(("shard", "ctx")),
            P(("shard", "ctx")),
            P(None, ("shard", "ctx"), "tp"),
            P(None, "tp"),
            P(("shard", "ctx"), "tp"),
            P(("shard", "ctx")),
            P(("shard", "ctx")),
            P(("shard", "ctx")),
            P(("shard", "ctx"), "tp"),
            P("tp"),
            P(("shard", "ctx"), "tp"),
            P(("shard", "ctx")),
        ),
        check_vma=False,
    )
```

```python
import functools
import math

import jax
import jax.numpy as jnp
from jax import lax
from jax.experimental import pallas as pl
from jax.experimental.pallas import tpu as pltpu
from jax.sharding import PartitionSpec as P

HD = 64


EPS = 1e-05
KAPPA = math.sqrt(2.0 / math.pi)


def normalize(row, gain, shift):
    center = jnp.mean(row, axis=-1, keepdims=True)
    centred = row - center
    inv_std = lax.rsqrt(jnp.mean(centred * centred, axis=-1, keepdims=True) + EPS)
    unit_rows = centred * inv_std
    return (unit_rows * gain + shift, unit_rows, inv_std)


def normalize_back(grad_out, unit_rows, inv_std, gain):
    scaled = grad_out * gain
    return inv_std * (
        scaled
        - jnp.mean(scaled, axis=-1, keepdims=True)
        - unit_rows * jnp.mean(scaled * unit_rows, axis=-1, keepdims=True)
    )


def gelu_pair(pre_act):
    inner = KAPPA * (pre_act + 0.044715 * pre_act * pre_act * pre_act)
    tanh_val = jnp.tanh(inner)
    value_out = 0.5 * pre_act * (1.0 + tanh_val)
    slope = 0.5 * (1.0 + tanh_val) + 0.5 * pre_act * (1.0 - tanh_val * tanh_val) * KAPPA * (
        1.0 + 3.0 * 0.044715 * pre_act * pre_act
    )
    return (value_out, slope)


def contract_last(left, right):
    return lax.dot_general(
        left, right, (((1,), (1,)), ((), ())), preferred_element_type=jnp.float32
    )


def contract_first(left, right):
    return lax.dot_general(
        left, right, (((0,), (0,)), ((), ())), preferred_element_type=jnp.float32
    )


MESH = pl.DeviceIdType.MESH
VMEM_SPEC = pl.BlockSpec(memory_space=pltpu.VMEM)


def remote(src, dst, send_sem, recv_sem, device):
    return pltpu.make_async_remote_copy(
        src_ref=src,
        dst_ref=dst,
        send_sem=send_sem,
        recv_sem=recv_sem,
        device_id=device,
        device_id_type=MESH,
    )


def greet(devices):
    barrier = pltpu.get_barrier_semaphore()
    for device in devices:
        pl.semaphore_signal(barrier, inc=1, device_id=device, device_id_type=MESH)
    pl.semaphore_wait(barrier, len(devices))


def params(collective_id):
    return pltpu.CompilerParams(
        collective_id=collective_id, has_side_effects=True, vmem_limit_bytes=48 * 2**20
    )


def dma_sems(*counts):
    return [pltpu.SemaphoreType.DMA((count,)) for count in counts]


def tp_kernel(n, x_ref, out_ref, recv, send_one, recv_one, send_two, recv_two):
    me = lax.axis_index("tp")
    rows = x_ref.shape[0] // n
    peers = [lax.rem(me + k, n) for k in range(1, n)]

    def share(index):
        return pl.ds(pl.multiple_of(index * rows, rows), rows)

    greet([{"tp": peer} for peer in peers])
    first = [
        remote(x_ref.at[share(peer)], recv.at[k], send_one.at[k], recv_one.at[k], {"tp": peer})
        for k, peer in enumerate(peers)
    ]
    for copy in first:
        copy.start()
    total = x_ref[share(me), :].astype(jnp.float32)
    for k, copy in enumerate(first):
        copy.wait_recv()
        total = total + recv[k].astype(jnp.float32)
    out_ref[share(me), :] = total.astype(out_ref.dtype)
    second = [
        remote(
            out_ref.at[share(me)], out_ref.at[share(me)], send_two.at[k], recv_two.at[k], {"tp": peer}
        )
        for k, peer in enumerate(peers)
    ]
    for copy in second:
        copy.start()
    for copy in first:
        copy.wait_send()
    for copy in second:
        copy.wait()


def sum_tp(part, n):
    part = part.astype(jnp.bfloat16)
    rows, width = part.shape
    total = pl.pallas_call(
        functools.partial(tp_kernel, n),
        out_shape=jax.ShapeDtypeStruct(part.shape, part.dtype),
        in_specs=[VMEM_SPEC],
        out_specs=VMEM_SPEC,
        scratch_shapes=[pltpu.VMEM((n - 1, rows // n, width), part.dtype)]
        + dma_sems(n - 1, n - 1, n - 1, n - 1),
        compiler_params=params(1),
        cost_estimate=pl.CostEstimate(flops=0, bytes_accessed=120_000_000, transcendentals=0),
        name="sum_tp",
    )(part)
    return total.astype(jnp.float32)


def group(shards, ctx):
    chips_y = ctx // 2
    place = lax.axis_index("ctx")
    core = lax.rem(place, 2)
    chip = place // 2
    if shards > 1:
        chip = chip + lax.axis_index("shard") * chips_y

    def device(index):
        where = {"ctx": lax.rem(index, chips_y) * 2 + core}
        if shards > 1:
            where["shard"] = index // chips_y
        return where

    return chip, core, device, {"ctx": place + 1 - 2 * core}


def gather_kernel(shards, ctx, x_ref, out_ref, own_sem, send_sem, recv_sem):
    chips = shards * ctx // 2
    chip, core, device, sibling = group(shards, ctx)
    other = 1 - core
    targets = [device(lax.rem(chip + k, chips)) for k in range(1, chips)]
    greet(targets + [sibling])
    mine = chip * 2 + core
    keep = pltpu.make_async_copy(x_ref, out_ref.at[mine], own_sem.at[0])
    keep.start()
    away = [
        remote(x_ref, out_ref.at[mine], send_sem.at[k], recv_sem.at[k], target)
        for k, target in enumerate(targets + [sibling])
    ]
    for copy in away:
        copy.start()
    onward = []
    for k in range(1, chips):
        away[k - 1].wait_recv()
        source = lax.rem(chip - k + chips, chips) * 2 + core
        copy = remote(
            out_ref.at[source],
            out_ref.at[source],
            send_sem.at[chips + k - 1],
            recv_sem.at[chips + k - 1],
            sibling,
        )
        copy.start()
        onward.append(copy)
    away[-1].wait_recv()
    for copy in onward:
        copy.wait()
    for copy in away:
        copy.wait_send()
    keep.wait()


def gather(block, shards, ctx, collective_id):
    count = shards * ctx
    return pl.pallas_call(
        functools.partial(gather_kernel, shards, ctx),
        out_shape=jax.ShapeDtypeStruct((count,) + block.shape, block.dtype),
        in_specs=[VMEM_SPEC],
        out_specs=VMEM_SPEC,
        scratch_shapes=dma_sems(1, count - 1, count - 1),
        compiler_params=params(collective_id),
        cost_estimate=pl.CostEstimate(flops=0, bytes_accessed=40_000_000, transcendentals=0),
        name="gather_blocks",
    )(block)


def scatter_kernel(shards, ctx, x_ref, out_ref, pair, held, send_sem, recv_sem, pair_send, pair_recv):
    chips = shards * ctx // 2
    chip, core, device, sibling = group(shards, ctx)
    other = 1 - core
    targets = [device(lax.rem(chip + k, chips)) for k in range(1, chips)]
    greet(targets + [sibling])
    order = [lax.rem(chip + k, chips) for k in range(1, chips)] + [chip]
    swaps = [
        remote(
            x_ref.at[owner * 2 + other], pair.at[k], pair_send.at[k], pair_recv.at[k], sibling
        )
        for k, owner in enumerate(order)
    ]
    for copy in swaps:
        copy.start()
    away = []
    for k, owner in enumerate(order):
        swaps[k].wait_recv()
        both = x_ref[owner * 2 + core].astype(jnp.float32) + pair[k].astype(jnp.float32)
        if k < chips - 1:
            pair[k] = both.astype(pair.dtype)
            copy = remote(pair.at[k], held.at[k], send_sem.at[k], recv_sem.at[k], targets[k])
            copy.start()
            away.append(copy)
        else:
            out_ref[...] = both
    for k, copy in enumerate(away):
        copy.wait_recv()
        out_ref[...] += held[k].astype(jnp.float32)
    for copy in away + swaps:
        copy.wait_send()


def scatter(blocks, shards, ctx, collective_id):
    count = shards * ctx
    chips = count // 2
    shape = blocks.shape[1:]
    return pl.pallas_call(
        functools.partial(scatter_kernel, shards, ctx),
        out_shape=jax.ShapeDtypeStruct(shape, jnp.float32),
        in_specs=[VMEM_SPEC],
        out_specs=VMEM_SPEC,
        scratch_shapes=[
            pltpu.VMEM((chips,) + shape, blocks.dtype),
            pltpu.VMEM((chips - 1,) + shape, blocks.dtype),
        ]
        + dma_sems(chips - 1, chips - 1, chips, chips),
        compiler_params=params(collective_id),
        cost_estimate=pl.CostEstimate(flops=0, bytes_accessed=40_000_000, transcendentals=0),
        name="scatter_blocks",
    )(blocks)


def small_kernel(shards, ctx, x_ref, out_ref, held, send_sem, recv_sem):
    count = shards * ctx
    me = lax.axis_index("shard") * ctx + lax.axis_index("ctx")
    peers = [lax.rem(me + k, count) for k in range(1, count)]
    targets = [{"shard": peer // ctx, "ctx": lax.rem(peer, ctx)} for peer in peers]
    greet(targets)
    copies = [
        remote(x_ref, held.at[k], send_sem.at[k], recv_sem.at[k], target)
        for k, target in enumerate(targets)
    ]
    for copy in copies:
        copy.start()
    out_ref[...] = x_ref[...]
    for k, copy in enumerate(copies):
        copy.wait_recv()
        out_ref[...] += held[k]
    for copy in copies:
        copy.wait_send()


def small_sum(part, shards, ctx, collective_id):
    count = shards * ctx
    return pl.pallas_call(
        functools.partial(small_kernel, shards, ctx),
        out_shape=jax.ShapeDtypeStruct(part.shape, part.dtype),
        in_specs=[VMEM_SPEC],
        out_specs=VMEM_SPEC,
        scratch_shapes=[pltpu.VMEM((count - 1,) + part.shape, part.dtype)]
        + dma_sems(count - 1, count - 1),
        compiler_params=params(collective_id),
        name="small_sum",
    )(part)


def on_device(
    shards,
    ctx,
    tp,
    hidden_in,
    lengths,
    cotangent,
    ln1_gain,
    ln1_bias,
    w_qkv,
    b_qv,
    w_out,
    b_out,
    ln2_gain,
    ln2_bias,
    w_up,
    b_up,
    w_down,
    b_down,
):
    groups, block_len, width = hidden_in.shape
    head_width = w_qkv.shape[2]
    heads_here = head_width // HD
    row_count = groups * block_len
    scale = 1.0 / math.sqrt(HD)
    rows_own = w_out.shape[0]
    vectors = jnp.stack([ln1_gain, ln1_bias, b_out, ln2_gain, ln2_bias, b_down], 1)
    packed_one = jnp.concatenate(
        [w_qkv[0], w_qkv[1], w_qkv[2], w_out, jnp.pad(vectors, ((0, 0), (0, 122)))], 1
    )
    packed_two = jnp.concatenate([w_up, w_down], 1)
    whole_one = gather(packed_one, shards, ctx, 2).reshape(-1, packed_one.shape[1])
    whole_two = lax.all_gather(packed_two, ("shard", "ctx"), axis=0, tiled=True)
    qkv_width = 3 * head_width
    qkv_full = whole_one[:, :qkv_width]
    out_full = whole_one[:, qkv_width : qkv_width + head_width]
    vec_wide = whole_one[:, qkv_width + head_width :].astype(jnp.float32).T
    up_full = whole_two[:, : w_up.shape[1]]
    down_full = whole_two[:, w_up.shape[1] :]
    gain_one = vec_wide[0]
    shift_one = vec_wide[1]
    bias_out = vec_wide[2]
    gain_two = vec_wide[3]
    shift_two = vec_wide[4]
    bias_down = vec_wide[5]
    ctx_index = lax.axis_index("ctx")
    positions = jnp.arange(block_len, dtype=jnp.int32) + ctx_index * block_len
    live_rows = (positions[None, :] < lengths[:, None]).reshape(row_count, 1)

    def allowed_mask(start, count):
        key_pos = start + jnp.arange(count, dtype=jnp.int32)
        causal = key_pos[None, None, None, :] <= positions[None, None, :, None]
        inside = key_pos[None, None, None, :] < lengths[:, None, None, None]
        return causal & inside

    inputs = hidden_in.reshape(row_count, width).astype(jnp.float32)
    normed_one, unit_one, inv_one = normalize(inputs, gain_one, shift_one)
    normed_bf = normed_one.astype(jnp.bfloat16)
    product = jnp.dot(normed_bf, qkv_full, preferred_element_type=jnp.float32)
    projected = [product[:, j * head_width : (j + 1) * head_width] for j in range(3)]
    query = (projected[0] + b_qv[0].astype(jnp.float32)).astype(jnp.bfloat16)
    keys_here = projected[1].astype(jnp.bfloat16).reshape(groups, block_len, head_width)
    values_here = (
        (projected[2] + b_qv[1].astype(jnp.float32))
        .astype(jnp.bfloat16)
        .reshape(groups, block_len, head_width)
    )
    query_heads = query.reshape(groups, block_len, heads_here, HD)

    kv_blocks = gather(
        jnp.concatenate([keys_here, values_here], -1).reshape(row_count, 2 * head_width), 1, ctx, 3
    )
    kv_whole = (
        kv_blocks.reshape(ctx, groups, block_len, 2 * head_width)
        .transpose(1, 0, 2, 3)
        .reshape(groups, ctx * block_len, 2 * head_width)
    )
    keys_whole, values_whole = kv_whole[..., :head_width], kv_whole[..., head_width:]

    def fold_keys(step_fn, init):
        return step_fn(init, (keys_whole, values_whole), jnp.int32(0))

    def piece_scores(piece, start):
        key_piece, value_piece = piece
        count = key_piece.shape[1]
        key_heads = key_piece.reshape(groups, count, heads_here, HD)
        value_heads = value_piece.reshape(groups, count, heads_here, HD)
        scores = (
            jnp.einsum(
                "sqhd,skhd->shqk", query_heads, key_heads, preferred_element_type=jnp.float32
            )
            * scale
        )
        allowed = allowed_mask(start, count)
        return (jnp.where(allowed, scores, -1e30), allowed, value_heads)

    def totals_step(carry, piece, start):
        top, total = carry
        scores, allowed, unused = piece_scores(piece, start)
        new_top = jnp.maximum(top, jnp.max(scores, axis=-1))
        weights = jnp.where(allowed, jnp.exp(scores - new_top[..., None]), 0.0)
        total = jnp.sum(weights, axis=-1)
        return (new_top, total)

    start_totals = (
        jnp.full((groups, heads_here, block_len), -1e30, jnp.float32),
        jnp.zeros((groups, heads_here, block_len), jnp.float32),
    )
    top, total = fold_keys(totals_step, start_totals)
    log_total = top + jnp.log(total)

    def values_step(accum, piece, start):
        scores, allowed, value_heads = piece_scores(piece, start)
        probs_piece = jnp.where(allowed, jnp.exp(scores - log_total[..., None]), 0.0).astype(
            jnp.bfloat16
        )
        return jnp.einsum(
            "shqk,skhd->sqhd", probs_piece, value_heads, preferred_element_type=jnp.float32
        )

    accum = fold_keys(values_step, jnp.zeros((groups, block_len, heads_here, HD), jnp.float32))
    attended_heads = accum.astype(jnp.bfloat16)
    attended = attended_heads.reshape(row_count, head_width)
    proj_sum = sum_tp(contract_last(attended, out_full), tp)
    resid = inputs + proj_sum + bias_out
    normed_two, unit_two, inv_two = normalize(resid, gain_two, shift_two)
    second_bf = normed_two.astype(jnp.bfloat16)
    pre_act = jnp.dot(second_bf, up_full, preferred_element_type=jnp.float32) + b_up.astype(
        jnp.float32
    )
    activ, slope = gelu_pair(pre_act)
    hidden = activ.astype(jnp.bfloat16)
    mlp_sum = lax.psum(contract_last(hidden, down_full).astype(jnp.bfloat16), "tp").astype(
        jnp.float32
    )
    result = jnp.where(live_rows, resid + mlp_sum + bias_down, 0.0)
    grad_rows = jnp.where(live_rows, cotangent.reshape(row_count, width).astype(jnp.float32), 0.0)
    grad_bf = grad_rows.astype(jnp.bfloat16)
    grad_bias_down = jnp.sum(grad_rows, axis=0)
    grad_down = contract_first(grad_bf, hidden)
    d_pre = jnp.dot(grad_bf, down_full, preferred_element_type=jnp.float32) * slope
    d_pre_bf = d_pre.astype(jnp.bfloat16)
    grad_bias_up = jnp.sum(d_pre, axis=0)
    grad_up = contract_first(second_bf, d_pre_bf)
    back_two = sum_tp(contract_last(d_pre_bf, up_full), tp)
    grad_gain_two = jnp.sum(back_two * unit_two, axis=0)
    grad_shift_two = jnp.sum(back_two, axis=0)
    d_resid = grad_rows + normalize_back(back_two, unit_two, inv_two, gain_two)
    d_resid_bf = d_resid.astype(jnp.bfloat16)
    grad_bias_out = jnp.sum(d_resid, axis=0)
    grad_out = contract_first(d_resid_bf, attended)
    d_attended = jnp.dot(d_resid_bf, out_full, preferred_element_type=jnp.float32).astype(
        jnp.bfloat16
    )
    seq_len = keys_whole.shape[1]
    key_heads = keys_whole.reshape(groups, seq_len, heads_here, HD)
    value_heads = values_whole.reshape(groups, seq_len, heads_here, HD)
    scores = (
        jnp.einsum("sqhd,skhd->shqk", query_heads, key_heads, preferred_element_type=jnp.float32)
        * scale
    )
    allowed = allowed_mask(0, seq_len)
    exact_probs = jnp.where(allowed, jnp.exp(scores - log_total[..., None]), 0.0)
    d_att_heads = d_attended.reshape(groups, block_len, heads_here, HD)
    delta = jnp.transpose(
        jnp.sum(d_att_heads.astype(jnp.float32) * attended_heads.astype(jnp.float32), axis=-1),
        (0, 2, 1),
    )
    d_probs = jnp.einsum(
        "sqhd,skhd->shqk", d_att_heads, value_heads, preferred_element_type=jnp.float32
    )
    d_scores = (exact_probs * (d_probs - delta[..., None])).astype(jnp.bfloat16)
    d_query = (
        jnp.einsum("shqk,skhd->sqhd", d_scores, key_heads, preferred_element_type=jnp.float32)
        * scale
    )
    probs_bf = exact_probs.astype(jnp.bfloat16)
    key_terms = (
        jnp.einsum("shqk,sqhd->skhd", d_scores, query_heads, preferred_element_type=jnp.float32)
        * scale
    )
    value_terms = jnp.einsum(
        "shqk,sqhd->skhd", probs_bf, d_att_heads, preferred_element_type=jnp.float32
    )
    kv_terms = jnp.concatenate(
        [
            key_terms.reshape(groups, seq_len, head_width).astype(jnp.bfloat16),
            value_terms.reshape(groups, seq_len, head_width).astype(jnp.bfloat16),
        ],
        -1,
    )
    kv_blocks_grad = (
        kv_terms.reshape(groups, ctx, block_len, 2 * head_width)
        .transpose(1, 0, 2, 3)
        .reshape(ctx, row_count, 2 * head_width)
    )
    kv_sum = scatter(kv_blocks_grad, 1, ctx, 4)
    d_keys, d_values = kv_sum[..., :head_width], kv_sum[..., head_width:]
    d_query_rows = d_query.reshape(row_count, head_width)
    d_value_rows = d_values.reshape(row_count, head_width)
    grad_bias_qv = jnp.stack([jnp.sum(d_query_rows, axis=0), jnp.sum(d_value_rows, axis=0)], 0)
    stacked = jnp.concatenate(
        [d_query_rows, d_keys, d_value_rows], 1
    ).astype(jnp.bfloat16)
    grad_qkv = contract_first(normed_bf, stacked)
    back_one = sum_tp(contract_last(stacked, qkv_full), tp)
    grad_gain_one = jnp.sum(back_one * unit_one, axis=0)
    grad_shift_one = jnp.sum(back_one, axis=0)
    d_inputs = d_resid + normalize_back(back_one, unit_one, inv_one, gain_one)
    vec_grads = jnp.concatenate(
        [
            grad_gain_one,
            grad_shift_one,
            grad_bias_out,
            grad_gain_two,
            grad_shift_two,
            grad_bias_down,
            grad_bias_qv.reshape(-1),
            grad_bias_up,
        ]
    )
    back_pair = jnp.concatenate([grad_qkv, grad_out], 1).astype(jnp.bfloat16)
    ffn_pair = jnp.concatenate([grad_up, grad_down], 1).astype(jnp.bfloat16)
    sum_ffn = lax.psum_scatter(
        ffn_pair, ("shard", "ctx"), scatter_dimension=0, tiled=True
    ).astype(jnp.float32)
    sum_back = lax.psum_scatter(
        back_pair, ("shard", "ctx"), scatter_dimension=0, tiled=True
    ).astype(jnp.float32)
    sum_qkv = jnp.stack(
        [sum_back[:, j * head_width : (j + 1) * head_width] for j in range(3)], 0
    )
    sum_out = sum_back[:, qkv_width:]
    sum_up, sum_down = sum_ffn[:, : w_up.shape[1]], sum_ffn[:, w_up.shape[1] :]
    all_vec = small_sum(vec_grads.reshape(-1, 128), shards, ctx, 5).reshape(-1)
    own = lax.axis_index(("shard", "ctx")) * rows_own
    sum_vec = lax.dynamic_slice(all_vec[: 6 * width].reshape(6, width), (0, own), (6, rows_own))
    bias_qv_sum = all_vec[6 * width : 6 * width + 2 * head_width].reshape(2, head_width)
    bias_up_sum = all_vec[6 * width + 2 * head_width :]
    return (
        result.reshape(groups, block_len, width),
        d_inputs.reshape(groups, block_len, width),
        sum_vec[0],
        sum_vec[1],
        sum_qkv,
        bias_qv_sum,
        sum_out,
        sum_vec[2],
        sum_vec[3],
        sum_vec[4],
        sum_up,
        bias_up_sum,
        sum_down,
        sum_vec[5],
    )


def solution(mesh):
    return jax.shard_map(
        functools.partial(
            on_device, mesh.shape["shard"], mesh.shape["ctx"], mesh.shape["tp"]
        ),
        mesh=mesh,
        in_specs=(
            P("shard", "ctx", None),
            P("shard"),
            P("shard", "ctx", None),
            P(("shard", "ctx")),
            P(("shard", "ctx")),
            P(None, ("shard", "ctx"), "tp"),
            P(None, "tp"),
            P(("shard", "ctx"), "tp"),
            P(("shard", "ctx")),
            P(("shard", "ctx")),
            P(("shard", "ctx")),
            P(("shard", "ctx"), "tp"),
            P("tp"),
            P(("shard", "ctx"), "tp"),
            P(("shard", "ctx")),
        ),
        out_specs=(
            P("shard", "ctx", None),
            P("shard", "ctx", None),
            P(("shard", "ctx")),
            P(("shard", "ctx")),
            P(None, ("shard", "ctx"), "tp"),
            P(None, "tp"),
            P(("shard", "ctx"), "tp"),
            P(("shard", "ctx")),
            P(("shard", "ctx")),
            P(("shard", "ctx")),
            P(("shard", "ctx"), "tp"),
            P("tp"),
            P(("shard", "ctx"), "tp"),
            P(("shard", "ctx")),
        ),
        check_vma=False,
    )
```

```python
import functools
import math

import jax
import jax.numpy as jnp
from jax import lax
from jax.experimental import pallas as pl
from jax.experimental.pallas import tpu as pltpu
from jax.sharding import PartitionSpec as P

HD = 64


EPS = 1e-05
KAPPA = math.sqrt(2.0 / math.pi)


def normalize(row, gain, shift):
    center = jnp.mean(row, axis=-1, keepdims=True)
    centred = row - center
    inv_std = lax.rsqrt(jnp.mean(centred * centred, axis=-1, keepdims=True) + EPS)
    unit_rows = centred * inv_std
    return (unit_rows * gain + shift, unit_rows, inv_std)


def normalize_back(grad_out, unit_rows, inv_std, gain):
    scaled = grad_out * gain
    return inv_std * (
        scaled
        - jnp.mean(scaled, axis=-1, keepdims=True)
        - unit_rows * jnp.mean(scaled * unit_rows, axis=-1, keepdims=True)
    )


def gelu_pair(pre_act):
    inner = KAPPA * (pre_act + 0.044715 * pre_act * pre_act * pre_act)
    tanh_val = jnp.tanh(inner)
    value_out = 0.5 * pre_act * (1.0 + tanh_val)
    slope = 0.5 * (1.0 + tanh_val) + 0.5 * pre_act * (1.0 - tanh_val * tanh_val) * KAPPA * (
        1.0 + 3.0 * 0.044715 * pre_act * pre_act
    )
    return (value_out, slope)


def contract_last(left, right):
    return lax.dot_general(
        left, right, (((1,), (1,)), ((), ())), preferred_element_type=jnp.float32
    )


def contract_first(left, right):
    return lax.dot_general(
        left, right, (((0,), (0,)), ((), ())), preferred_element_type=jnp.float32
    )


MESH = pl.DeviceIdType.MESH
VMEM_SPEC = pl.BlockSpec(memory_space=pltpu.VMEM)


def remote(src, dst, send_sem, recv_sem, device):
    return pltpu.make_async_remote_copy(
        src_ref=src,
        dst_ref=dst,
        send_sem=send_sem,
        recv_sem=recv_sem,
        device_id=device,
        device_id_type=MESH,
    )


def greet(devices):
    barrier = pltpu.get_barrier_semaphore()
    for device in devices:
        pl.semaphore_signal(barrier, inc=1, device_id=device, device_id_type=MESH)
    pl.semaphore_wait(barrier, len(devices))


def params(collective_id):
    return pltpu.CompilerParams(
        collective_id=collective_id, has_side_effects=True, vmem_limit_bytes=48 * 2**20
    )


def dma_sems(*counts):
    return [pltpu.SemaphoreType.DMA((count,)) for count in counts]


def tp_peers(n):
    me = lax.axis_index("tp")
    return me, [lax.rem(me + k, n) for k in range(1, n)]


def tp_steps(n, x_ref, out_ref, recv, send_one, recv_one, send_two, recv_two):
    me, peers = tp_peers(n)
    rows = x_ref.shape[0] // n

    def share(index):
        return pl.ds(pl.multiple_of(index * rows, rows), rows)

    first = [
        remote(x_ref.at[share(peer)], recv.at[k], send_one.at[k], recv_one.at[k], {"tp": peer})
        for k, peer in enumerate(peers)
    ]
    for copy in first:
        copy.start()
    yield
    total = x_ref[share(me), :].astype(jnp.float32)
    for k, copy in enumerate(first):
        copy.wait_recv()
        total = total + recv[k].astype(jnp.float32)
    out_ref[share(me), :] = total.astype(out_ref.dtype)
    second = [
        remote(
            out_ref.at[share(me)], out_ref.at[share(me)], send_two.at[k], recv_two.at[k], {"tp": peer}
        )
        for k, peer in enumerate(peers)
    ]
    for copy in second:
        copy.start()
    yield
    for copy in first:
        copy.wait_send()
    for copy in second:
        copy.wait()
    yield


def tp_gather_kernel(n, x_ref, out_ref, own_sem, send_sem, recv_sem):
    me = lax.axis_index("tp")
    width = x_ref.shape[1]
    peers = [lax.rem(me + k, n) for k in range(1, n)]
    mine = out_ref.at[:, pl.ds(pl.multiple_of(me * width, width), width)]
    greet([{"tp": peer} for peer in peers])
    copies = [
        remote(x_ref, mine, send_sem.at[k], recv_sem.at[k], {"tp": peer})
        for k, peer in enumerate(peers)
    ]
    for copy in copies:
        copy.start()
    keep = pltpu.make_async_copy(x_ref, mine, own_sem.at[0])
    keep.start()
    for copy in copies:
        copy.wait()
    keep.wait()


def gather_tp(block, n):
    rows, width = block.shape
    return pl.pallas_call(
        functools.partial(tp_gather_kernel, n),
        out_shape=jax.ShapeDtypeStruct((rows, n * width), block.dtype),
        in_specs=[VMEM_SPEC],
        out_specs=VMEM_SPEC,
        scratch_shapes=dma_sems(1, n - 1, n - 1),
        compiler_params=params(7),
        cost_estimate=pl.CostEstimate(flops=0, bytes_accessed=60_000_000, transcendentals=0),
        name="gather_tp",
    )(block)


def group(shards, ctx):
    chips_y = ctx // 2
    place = lax.axis_index("ctx")
    core = lax.rem(place, 2)
    chip = place // 2
    if shards > 1:
        chip = chip + lax.axis_index("shard") * chips_y

    def device(index):
        where = {"ctx": lax.rem(index, chips_y) * 2 + core}
        if shards > 1:
            where["shard"] = index // chips_y
        return where

    return chip, core, device, {"ctx": place + 1 - 2 * core}


def gather_kernel(shards, ctx, x_ref, out_ref, own_sem, send_sem, recv_sem):
    chips = shards * ctx // 2
    chip, core, device, sibling = group(shards, ctx)
    other = 1 - core
    targets = [device(lax.rem(chip + k, chips)) for k in range(1, chips)]
    greet(targets + [sibling])
    mine = chip * 2 + core
    keep = pltpu.make_async_copy(x_ref, out_ref.at[mine], own_sem.at[0])
    keep.start()
    away = [
        remote(x_ref, out_ref.at[mine], send_sem.at[k], recv_sem.at[k], target)
        for k, target in enumerate(targets + [sibling])
    ]
    for copy in away:
        copy.start()
    onward = []
    for k in range(1, chips):
        away[k - 1].wait_recv()
        source = lax.rem(chip - k + chips, chips) * 2 + core
        copy = remote(
            out_ref.at[source],
            out_ref.at[source],
            send_sem.at[chips + k - 1],
            recv_sem.at[chips + k - 1],
            sibling,
        )
        copy.start()
        onward.append(copy)
    away[-1].wait_recv()
    for copy in onward:
        copy.wait()
    for copy in away:
        copy.wait_send()
    keep.wait()


def gather(block, shards, ctx, collective_id):
    count = shards * ctx
    return pl.pallas_call(
        functools.partial(gather_kernel, shards, ctx),
        out_shape=jax.ShapeDtypeStruct((count,) + block.shape, block.dtype),
        in_specs=[VMEM_SPEC],
        out_specs=VMEM_SPEC,
        scratch_shapes=dma_sems(1, count - 1, count - 1),
        compiler_params=params(collective_id),
        cost_estimate=pl.CostEstimate(flops=0, bytes_accessed=40_000_000, transcendentals=0),
        name="gather_blocks",
    )(block)


def scatter_targets(shards, ctx):
    chips = shards * ctx // 2
    chip, core, device, sibling = group(shards, ctx)
    return [device(lax.rem(chip + k, chips)) for k in range(1, chips)] + [sibling]


def scatter_steps(
    shards, ctx, x_ref, out_ref, pair, held, send_sem, recv_sem, pair_send, pair_recv
):
    chips = shards * ctx // 2
    chip, core, device, sibling = group(shards, ctx)
    other = 1 - core
    targets = scatter_targets(shards, ctx)
    order = [lax.rem(chip + k, chips) for k in range(1, chips)] + [chip]
    swaps = [
        remote(
            x_ref.at[owner * 2 + other], pair.at[k], pair_send.at[k], pair_recv.at[k], sibling
        )
        for k, owner in enumerate(order)
    ]
    for copy in swaps:
        copy.start()
    yield
    away = []
    for k, owner in enumerate(order):
        swaps[k].wait_recv()
        both = x_ref[owner * 2 + core].astype(jnp.float32) + pair[k].astype(jnp.float32)
        if k < chips - 1:
            pair[k] = both.astype(pair.dtype)
            copy = remote(pair.at[k], held.at[k], send_sem.at[k], recv_sem.at[k], targets[k])
            copy.start()
            away.append(copy)
        else:
            out_ref[...] = both
    yield
    for k, copy in enumerate(away):
        copy.wait_recv()
        out_ref[...] += held[k].astype(jnp.float32)
    for copy in away + swaps:
        copy.wait_send()
    yield


def scatter_kernel(shards, ctx, x_ref, out_ref, *scratch):
    greet(scatter_targets(shards, ctx))
    for _ in scatter_steps(shards, ctx, x_ref, out_ref, *scratch):
        pass


def scatter_scratch(blocks, chips):
    shape = blocks.shape[1:]
    return [
        pltpu.VMEM((chips,) + shape, blocks.dtype),
        pltpu.VMEM((chips - 1,) + shape, blocks.dtype),
    ] + dma_sems(chips - 1, chips - 1, chips, chips)


def both_kernel(n, shards, ctx, part_ref, blocks_ref, total_ref, own_ref, *scratch):
    me, peers = tp_peers(n)
    greet([{"tp": peer} for peer in peers] + scatter_targets(shards, ctx))
    along = tp_steps(n, part_ref, total_ref, *scratch[:5])
    across = scatter_steps(shards, ctx, blocks_ref, own_ref, *scratch[5:])
    next(along)
    next(across)
    next(across)
    next(along)
    next(across)
    next(along)


def sum_and_scatter(part, blocks, n, shards, ctx, collective_id):
    rows, width = part.shape
    blocks = blocks.reshape(shards * ctx, -1, blocks.shape[1])
    total, own = pl.pallas_call(
        functools.partial(both_kernel, n, shards, ctx),
        out_shape=(
            jax.ShapeDtypeStruct(part.shape, part.dtype),
            jax.ShapeDtypeStruct(blocks.shape[1:], jnp.float32),
        ),
        in_specs=[VMEM_SPEC] * 2,
        out_specs=(VMEM_SPEC,) * 2,
        scratch_shapes=[pltpu.VMEM((n - 1, rows // n, width), part.dtype)]
        + dma_sems(n - 1, n - 1, n - 1, n - 1)
        + scatter_scratch(blocks, shards * ctx // 2),
        compiler_params=params(collective_id),
        cost_estimate=pl.CostEstimate(flops=0, bytes_accessed=120_000_000, transcendentals=0),
        name="sum_and_scatter",
    )(part, blocks)
    return total.astype(jnp.float32), own


def scatter(blocks, shards, ctx, collective_id):
    count = shards * ctx
    chips = count // 2
    shape = blocks.shape[1:]
    return pl.pallas_call(
        functools.partial(scatter_kernel, shards, ctx),
        out_shape=jax.ShapeDtypeStruct(shape, jnp.float32),
        in_specs=[VMEM_SPEC],
        out_specs=VMEM_SPEC,
        scratch_shapes=scatter_scratch(blocks, chips),
        compiler_params=params(collective_id),
        cost_estimate=pl.CostEstimate(flops=0, bytes_accessed=1000, transcendentals=0),
        name="scatter_blocks",
    )(blocks)


def small_kernel(shards, ctx, x_ref, out_ref, held, send_sem, recv_sem):
    count = shards * ctx
    me = lax.axis_index("shard") * ctx + lax.axis_index("ctx")
    peers = [lax.rem(me + k, count) for k in range(1, count)]
    targets = [{"shard": peer // ctx, "ctx": lax.rem(peer, ctx)} for peer in peers]
    greet(targets)
    copies = [
        remote(x_ref, held.at[k], send_sem.at[k], recv_sem.at[k], target)
        for k, target in enumerate(targets)
    ]
    for copy in copies:
        copy.start()
    out_ref[...] = x_ref[...]
    for k, copy in enumerate(copies):
        copy.wait_recv()
        out_ref[...] += held[k]
    for copy in copies:
        copy.wait_send()


def small_sum(part, shards, ctx, collective_id):
    count = shards * ctx
    return pl.pallas_call(
        functools.partial(small_kernel, shards, ctx),
        out_shape=jax.ShapeDtypeStruct(part.shape, part.dtype),
        in_specs=[VMEM_SPEC],
        out_specs=VMEM_SPEC,
        scratch_shapes=[pltpu.VMEM((count - 1,) + part.shape, part.dtype)]
        + dma_sems(count - 1, count - 1),
        compiler_params=params(collective_id),
        name="small_sum",
    )(part)


def on_device(
    shards,
    ctx,
    tp,
    hidden_in,
    lengths,
    cotangent,
    ln1_gain,
    ln1_bias,
    w_qkv,
    b_qv,
    w_out,
    b_out,
    ln2_gain,
    ln2_bias,
    w_up,
    b_up,
    w_down,
    b_down,
):
    groups, block_len, width = hidden_in.shape
    head_width = w_qkv.shape[2]
    heads_here = head_width // HD
    row_count = groups * block_len
    scale = 1.0 / math.sqrt(HD)
    rows_own = w_out.shape[0]
    vectors = jnp.stack([ln1_gain, ln1_bias, b_out, ln2_gain, ln2_bias, b_down], 1)
    packed_one = jnp.concatenate(
        [w_qkv[0], w_qkv[1], w_qkv[2], w_out, jnp.pad(vectors, ((0, 0), (0, 122)))], 1
    )
    packed_two = jnp.concatenate([w_up, w_down], 1)
    whole_one = gather(packed_one, shards, ctx, 2).reshape(-1, packed_one.shape[1])
    packed_two, whole_one = lax.optimization_barrier((packed_two, whole_one))
    whole_two = lax.all_gather(packed_two, ("shard", "ctx"), axis=0, tiled=True)
    qkv_width = 3 * head_width
    qkv_full = whole_one[:, :qkv_width]
    out_full = whole_one[:, qkv_width : qkv_width + head_width]
    out_wide = lax.all_gather(out_full, "tp", axis=1, tiled=True)
    vec_wide = whole_one[:, qkv_width + head_width :].astype(jnp.float32).T
    up_full = whole_two[:, : w_up.shape[1]]
    down_full = whole_two[:, w_up.shape[1] :]
    gain_one = vec_wide[0]
    shift_one = vec_wide[1]
    bias_out = vec_wide[2]
    gain_two = vec_wide[3]
    shift_two = vec_wide[4]
    bias_down = vec_wide[5]
    ctx_index = lax.axis_index("ctx")
    positions = jnp.arange(block_len, dtype=jnp.int32) + ctx_index * block_len
    live_rows = (positions[None, :] < lengths[:, None]).reshape(row_count, 1)

    def allowed_mask(start, count):
        key_pos = start + jnp.arange(count, dtype=jnp.int32)
        causal = key_pos[None, None, None, :] <= positions[None, None, :, None]
        inside = key_pos[None, None, None, :] < lengths[:, None, None, None]
        return causal & inside

    inputs = hidden_in.reshape(row_count, width).astype(jnp.float32)
    normed_one, unit_one, inv_one = normalize(inputs, gain_one, shift_one)
    normed_bf = normed_one.astype(jnp.bfloat16)
    product = jnp.dot(normed_bf, qkv_full, preferred_element_type=jnp.float32)
    projected = [product[:, j * head_width : (j + 1) * head_width] for j in range(3)]
    query = (projected[0] + b_qv[0].astype(jnp.float32)).astype(jnp.bfloat16)
    keys_here = projected[1].astype(jnp.bfloat16).reshape(groups, block_len, head_width)
    values_here = (
        (projected[2] + b_qv[1].astype(jnp.float32))
        .astype(jnp.bfloat16)
        .reshape(groups, block_len, head_width)
    )
    query_heads = query.reshape(groups, block_len, heads_here, HD)

    kv_blocks = gather(
        jnp.concatenate([keys_here, values_here], -1).reshape(row_count, 2 * head_width), 1, ctx, 3
    )
    kv_whole = (
        kv_blocks.reshape(ctx, groups, block_len, 2 * head_width)
        .transpose(1, 0, 2, 3)
        .reshape(groups, ctx * block_len, 2 * head_width)
    )
    keys_whole, values_whole = kv_whole[..., :head_width], kv_whole[..., head_width:]

    def fold_keys(step_fn, init):
        return step_fn(init, (keys_whole, values_whole), jnp.int32(0))

    def piece_scores(piece, start):
        key_piece, value_piece = piece
        count = key_piece.shape[1]
        key_heads = key_piece.reshape(groups, count, heads_here, HD)
        value_heads = value_piece.reshape(groups, count, heads_here, HD)
        scores = (
            jnp.einsum(
                "sqhd,skhd->shqk", query_heads, key_heads, preferred_element_type=jnp.float32
            )
            * scale
        )
        allowed = allowed_mask(start, count)
        return (jnp.where(allowed, scores, -1e30), allowed, value_heads)

    def totals_step(carry, piece, start):
        top, total = carry
        scores, allowed, unused = piece_scores(piece, start)
        new_top = jnp.maximum(top, jnp.max(scores, axis=-1))
        weights = jnp.where(allowed, jnp.exp(scores - new_top[..., None]), 0.0)
        total = jnp.sum(weights, axis=-1)
        return (new_top, total)

    start_totals = (
        jnp.full((groups, heads_here, block_len), -1e30, jnp.float32),
        jnp.zeros((groups, heads_here, block_len), jnp.float32),
    )
    top, total = fold_keys(totals_step, start_totals)
    log_total = top + jnp.log(total)

    def values_step(accum, piece, start):
        scores, allowed, value_heads = piece_scores(piece, start)
        probs_piece = jnp.where(allowed, jnp.exp(scores - log_total[..., None]), 0.0).astype(
            jnp.bfloat16
        )
        return jnp.einsum(
            "shqk,skhd->sqhd", probs_piece, value_heads, preferred_element_type=jnp.float32
        )

    accum = fold_keys(values_step, jnp.zeros((groups, block_len, heads_here, HD), jnp.float32))
    attended_heads = accum.astype(jnp.bfloat16)
    attended = attended_heads.reshape(row_count, head_width)
    proj_sum = contract_last(gather_tp(attended, tp), out_wide)
    resid = inputs + proj_sum + bias_out
    normed_two, unit_two, inv_two = normalize(resid, gain_two, shift_two)
    second_bf = normed_two.astype(jnp.bfloat16)
    pre_act = jnp.dot(second_bf, up_full, preferred_element_type=jnp.float32) + b_up.astype(
        jnp.float32
    )
    activ, slope = gelu_pair(pre_act)
    hidden = activ.astype(jnp.bfloat16)
    grad_rows = jnp.where(live_rows, cotangent.reshape(row_count, width).astype(jnp.float32), 0.0)
    grad_bf = grad_rows.astype(jnp.bfloat16)
    grad_bias_down = jnp.sum(grad_rows, axis=0)
    grad_down = contract_first(grad_bf, hidden)
    d_pre = jnp.dot(grad_bf, down_full, preferred_element_type=jnp.float32) * slope
    d_pre_bf = d_pre.astype(jnp.bfloat16)
    grad_bias_up = jnp.sum(d_pre, axis=0)
    grad_up = contract_first(second_bf, d_pre_bf)
    ffn_pair = jnp.concatenate(
        [grad_up.astype(jnp.bfloat16), grad_down.astype(jnp.bfloat16)], 1
    )
    back_part = contract_last(d_pre_bf, up_full).astype(jnp.bfloat16)
    back_two, sum_ffn = sum_and_scatter(back_part, ffn_pair, tp, shards, ctx, 1)
    mlp_part = contract_last(hidden, down_full).astype(jnp.bfloat16)
    mlp_part, back_two = lax.optimization_barrier((mlp_part, back_two))
    mlp_sum = lax.psum(mlp_part, "tp")
    grad_gain_two = jnp.sum(back_two * unit_two, axis=0)
    grad_shift_two = jnp.sum(back_two, axis=0)
    d_resid = grad_rows + normalize_back(back_two, unit_two, inv_two, gain_two)
    d_resid_bf = d_resid.astype(jnp.bfloat16)
    grad_bias_out = jnp.sum(d_resid, axis=0)
    grad_out = contract_first(d_resid_bf, attended)
    d_attended = jnp.dot(d_resid_bf, out_full, preferred_element_type=jnp.float32).astype(
        jnp.bfloat16
    )
    seq_len = keys_whole.shape[1]
    key_heads = keys_whole.reshape(groups, seq_len, heads_here, HD)
    value_heads = values_whole.reshape(groups, seq_len, heads_here, HD)
    scores = (
        jnp.einsum("sqhd,skhd->shqk", query_heads, key_heads, preferred_element_type=jnp.float32)
        * scale
    )
    allowed = allowed_mask(0, seq_len)
    exact_probs = jnp.where(allowed, jnp.exp(scores - log_total[..., None]), 0.0)
    d_att_heads = d_attended.reshape(groups, block_len, heads_here, HD)
    delta = jnp.transpose(
        jnp.sum(d_att_heads.astype(jnp.float32) * attended_heads.astype(jnp.float32), axis=-1),
        (0, 2, 1),
    )
    d_probs = jnp.einsum(
        "sqhd,skhd->shqk", d_att_heads, value_heads, preferred_element_type=jnp.float32
    )
    d_scores = (exact_probs * (d_probs - delta[..., None])).astype(jnp.bfloat16)
    d_query = (
        jnp.einsum("shqk,skhd->sqhd", d_scores, key_heads, preferred_element_type=jnp.float32)
        * scale
    )
    probs_bf = exact_probs.astype(jnp.bfloat16)
    key_terms = (
        jnp.einsum("shqk,sqhd->skhd", d_scores, query_heads, preferred_element_type=jnp.float32)
        * scale
    )
    value_terms = jnp.einsum(
        "shqk,sqhd->skhd", probs_bf, d_att_heads, preferred_element_type=jnp.float32
    )
    kv_terms = jnp.concatenate(
        [
            key_terms.reshape(groups, seq_len, head_width).astype(jnp.bfloat16),
            value_terms.reshape(groups, seq_len, head_width).astype(jnp.bfloat16),
        ],
        -1,
    )
    kv_blocks_grad = (
        kv_terms.reshape(groups, ctx, block_len, 2 * head_width)
        .transpose(1, 0, 2, 3)
        .reshape(ctx, row_count, 2 * head_width)
    )
    kv_sum = scatter(kv_blocks_grad, 1, ctx, 4)
    d_keys, d_values = kv_sum[..., :head_width], kv_sum[..., head_width:]
    d_query_rows = d_query.reshape(row_count, head_width)
    d_value_rows = d_values.reshape(row_count, head_width)
    grad_bias_qv = jnp.stack([jnp.sum(d_query_rows, axis=0), jnp.sum(d_value_rows, axis=0)], 0)
    stacked = jnp.concatenate(
        [d_query_rows, d_keys, d_value_rows], 1
    ).astype(jnp.bfloat16)
    grad_qkv = contract_first(normed_bf, stacked)
    back_pair = jnp.concatenate(
        [grad_qkv.astype(jnp.bfloat16), grad_out.astype(jnp.bfloat16)], 1
    )
    first_part = contract_last(stacked, qkv_full).astype(jnp.bfloat16)
    mlp_sum, first_part = lax.optimization_barrier((mlp_sum, first_part))
    result = jnp.where(live_rows, resid + mlp_sum.astype(jnp.float32) + bias_down, 0.0)
    back_one, sum_back = sum_and_scatter(first_part, back_pair, tp, shards, ctx, 6)
    grad_gain_one = jnp.sum(back_one * unit_one, axis=0)
    grad_shift_one = jnp.sum(back_one, axis=0)
    d_inputs = d_resid + normalize_back(back_one, unit_one, inv_one, gain_one)
    vec_grads = jnp.concatenate(
        [
            grad_gain_one,
            grad_shift_one,
            grad_bias_out,
            grad_gain_two,
            grad_shift_two,
            grad_bias_down,
            grad_bias_qv.reshape(-1),
            grad_bias_up,
        ]
    )
    sum_qkv = jnp.stack(
        [sum_back[:, j * head_width : (j + 1) * head_width] for j in range(3)], 0
    )
    sum_out = sum_back[:, qkv_width:]
    sum_up, sum_down = sum_ffn[:, : w_up.shape[1]], sum_ffn[:, w_up.shape[1] :]
    all_vec = small_sum(vec_grads.reshape(-1, 128), shards, ctx, 5).reshape(-1)
    own = lax.axis_index(("shard", "ctx")) * rows_own
    sum_vec = lax.dynamic_slice(all_vec[: 6 * width].reshape(6, width), (0, own), (6, rows_own))
    bias_qv_sum = all_vec[6 * width : 6 * width + 2 * head_width].reshape(2, head_width)
    bias_up_sum = all_vec[6 * width + 2 * head_width :]
    return (
        result.reshape(groups, block_len, width),
        d_inputs.reshape(groups, block_len, width),
        sum_vec[0],
        sum_vec[1],
        sum_qkv,
        bias_qv_sum,
        sum_out,
        sum_vec[2],
        sum_vec[3],
        sum_vec[4],
        sum_up,
        bias_up_sum,
        sum_down,
        sum_vec[5],
    )


def solution(mesh):
    return jax.shard_map(
        functools.partial(
            on_device, mesh.shape["shard"], mesh.shape["ctx"], mesh.shape["tp"]
        ),
        mesh=mesh,
        in_specs=(
            P("shard", "ctx", None),
            P("shard"),
            P("shard", "ctx", None),
            P(("shard", "ctx")),
            P(("shard", "ctx")),
            P(None, ("shard", "ctx"), "tp"),
            P(None, "tp"),
            P(("shard", "ctx"), "tp"),
            P(("shard", "ctx")),
            P(("shard", "ctx")),
            P(("shard", "ctx")),
            P(("shard", "ctx"), "tp"),
            P("tp"),
            P(("shard", "ctx"), "tp"),
            P(("shard", "ctx")),
        ),
        out_specs=(
            P("shard", "ctx", None),
            P("shard", "ctx", None),
            P(("shard", "ctx")),
            P(("shard", "ctx")),
            P(None, ("shard", "ctx"), "tp"),
            P(None, "tp"),
            P(("shard", "ctx"), "tp"),
            P(("shard", "ctx")),
            P(("shard", "ctx")),
            P(("shard", "ctx")),
            P(("shard", "ctx"), "tp"),
            P("tp"),
            P(("shard", "ctx"), "tp"),
            P(("shard", "ctx")),
        ),
        check_vma=False,
    )
```

```python
import functools
import math

import jax
import jax.numpy as jnp
from jax import lax
from jax.experimental import pallas as pl
from jax.experimental.pallas import tpu as pltpu
from jax.sharding import PartitionSpec as P

HD = 64


EPS = 1e-05
KAPPA = math.sqrt(2.0 / math.pi)


def normalize(row, gain, shift):
    center = jnp.mean(row, axis=-1, keepdims=True)
    centred = row - center
    inv_std = lax.rsqrt(jnp.mean(centred * centred, axis=-1, keepdims=True) + EPS)
    unit_rows = centred * inv_std
    return (unit_rows * gain + shift, unit_rows, inv_std)


def normalize_back(grad_out, unit_rows, inv_std, gain):
    scaled = grad_out * gain
    return inv_std * (
        scaled
        - jnp.mean(scaled, axis=-1, keepdims=True)
        - unit_rows * jnp.mean(scaled * unit_rows, axis=-1, keepdims=True)
    )


def gelu_pair(pre_act):
    inner = KAPPA * (pre_act + 0.044715 * pre_act * pre_act * pre_act)
    tanh_val = jnp.tanh(inner)
    value_out = 0.5 * pre_act * (1.0 + tanh_val)
    slope = 0.5 * (1.0 + tanh_val) + 0.5 * pre_act * (1.0 - tanh_val * tanh_val) * KAPPA * (
        1.0 + 3.0 * 0.044715 * pre_act * pre_act
    )
    return (value_out, slope)


def contract_last(left, right):
    return lax.dot_general(
        left, right, (((1,), (1,)), ((), ())), preferred_element_type=jnp.float32
    )


def contract_first(left, right):
    return lax.dot_general(
        left, right, (((0,), (0,)), ((), ())), preferred_element_type=jnp.float32
    )


MESH = pl.DeviceIdType.MESH
VMEM_SPEC = pl.BlockSpec(memory_space=pltpu.VMEM)


def remote(src, dst, send_sem, recv_sem, device):
    return pltpu.make_async_remote_copy(
        src_ref=src,
        dst_ref=dst,
        send_sem=send_sem,
        recv_sem=recv_sem,
        device_id=device,
        device_id_type=MESH,
    )


def greet(devices):
    barrier = pltpu.get_barrier_semaphore()
    for device in devices:
        pl.semaphore_signal(barrier, inc=1, device_id=device, device_id_type=MESH)
    pl.semaphore_wait(barrier, len(devices))


def params(collective_id):
    return pltpu.CompilerParams(
        collective_id=collective_id, has_side_effects=True, vmem_limit_bytes=48 * 2**20
    )


def dma_sems(*counts):
    return [pltpu.SemaphoreType.DMA((count,)) for count in counts]


def tp_peers(n):
    me = lax.axis_index("tp")
    return me, [lax.rem(me + k, n) for k in range(1, n)]


def tp_steps(n, x_ref, out_ref, recv, send_one, recv_one, send_two, recv_two):
    me, peers = tp_peers(n)
    rows = x_ref.shape[0] // n

    def share(index):
        return pl.ds(pl.multiple_of(index * rows, rows), rows)

    first = [
        remote(x_ref.at[share(peer)], recv.at[k], send_one.at[k], recv_one.at[k], {"tp": peer})
        for k, peer in enumerate(peers)
    ]
    for copy in first:
        copy.start()
    yield
    total = x_ref[share(me), :].astype(jnp.float32)
    for k, copy in enumerate(first):
        copy.wait_recv()
        total = total + recv[k].astype(jnp.float32)
    out_ref[share(me), :] = total.astype(out_ref.dtype)
    second = [
        remote(
            out_ref.at[share(me)], out_ref.at[share(me)], send_two.at[k], recv_two.at[k], {"tp": peer}
        )
        for k, peer in enumerate(peers)
    ]
    for copy in second:
        copy.start()
    yield
    for copy in first:
        copy.wait_send()
    for copy in second:
        copy.wait()
    yield


def tp_gather_kernel(n, x_ref, out_ref, own_sem, send_sem, recv_sem):
    me = lax.axis_index("tp")
    width = x_ref.shape[1]
    peers = [lax.rem(me + k, n) for k in range(1, n)]
    mine = out_ref.at[:, pl.ds(pl.multiple_of(me * width, width), width)]
    greet([{"tp": peer} for peer in peers])
    copies = [
        remote(x_ref, mine, send_sem.at[k], recv_sem.at[k], {"tp": peer})
        for k, peer in enumerate(peers)
    ]
    for copy in copies:
        copy.start()
    keep = pltpu.make_async_copy(x_ref, mine, own_sem.at[0])
    keep.start()
    for copy in copies:
        copy.wait()
    keep.wait()


def gather_tp(block, n):
    rows, width = block.shape
    return pl.pallas_call(
        functools.partial(tp_gather_kernel, n),
        out_shape=jax.ShapeDtypeStruct((rows, n * width), block.dtype),
        in_specs=[VMEM_SPEC],
        out_specs=VMEM_SPEC,
        scratch_shapes=dma_sems(1, n - 1, n - 1),
        compiler_params=params(7),
        cost_estimate=pl.CostEstimate(flops=0, bytes_accessed=60_000_000, transcendentals=0),
        name="gather_tp",
    )(block)


def group(shards, ctx):
    chips_y = ctx // 2
    place = lax.axis_index("ctx")
    core = lax.rem(place, 2)
    chip = place // 2
    if shards > 1:
        chip = chip + lax.axis_index("shard") * chips_y

    def device(index):
        where = {"ctx": lax.rem(index, chips_y) * 2 + core}
        if shards > 1:
            where["shard"] = index // chips_y
        return where

    return chip, core, device, {"ctx": place + 1 - 2 * core}


def gather_kernel(shards, ctx, x_ref, out_ref, own_sem, send_sem, recv_sem):
    chips = shards * ctx // 2
    chip, core, device, sibling = group(shards, ctx)
    other = 1 - core
    targets = [device(lax.rem(chip + k, chips)) for k in range(1, chips)]
    greet(targets + [sibling])
    mine = chip * 2 + core
    keep = pltpu.make_async_copy(x_ref, out_ref.at[mine], own_sem.at[0])
    keep.start()
    away = [
        remote(x_ref, out_ref.at[mine], send_sem.at[k], recv_sem.at[k], target)
        for k, target in enumerate(targets + [sibling])
    ]
    for copy in away:
        copy.start()
    onward = []
    for k in range(1, chips):
        away[k - 1].wait_recv()
        source = lax.rem(chip - k + chips, chips) * 2 + core
        copy = remote(
            out_ref.at[source],
            out_ref.at[source],
            send_sem.at[chips + k - 1],
            recv_sem.at[chips + k - 1],
            sibling,
        )
        copy.start()
        onward.append(copy)
    away[-1].wait_recv()
    for copy in onward:
        copy.wait()
    for copy in away:
        copy.wait_send()
    keep.wait()


def gather(block, shards, ctx, collective_id):
    count = shards * ctx
    return pl.pallas_call(
        functools.partial(gather_kernel, shards, ctx),
        out_shape=jax.ShapeDtypeStruct((count,) + block.shape, block.dtype),
        in_specs=[VMEM_SPEC],
        out_specs=VMEM_SPEC,
        scratch_shapes=dma_sems(1, count - 1, count - 1),
        compiler_params=params(collective_id),
        cost_estimate=pl.CostEstimate(flops=0, bytes_accessed=40_000_000, transcendentals=0),
        name="gather_blocks",
    )(block)


def scatter_targets(shards, ctx):
    chips = shards * ctx // 2
    chip, core, device, sibling = group(shards, ctx)
    return [device(lax.rem(chip + k, chips)) for k in range(1, chips)] + [sibling]


def scatter_steps(
    shards, ctx, x_ref, out_ref, pair, held, send_sem, recv_sem, pair_send, pair_recv
):
    chips = shards * ctx // 2
    chip, core, device, sibling = group(shards, ctx)
    other = 1 - core
    targets = scatter_targets(shards, ctx)
    order = [lax.rem(chip + k, chips) for k in range(1, chips)] + [chip]
    swaps = [
        remote(
            x_ref.at[owner * 2 + other], pair.at[k], pair_send.at[k], pair_recv.at[k], sibling
        )
        for k, owner in enumerate(order)
    ]
    for copy in swaps:
        copy.start()
    yield
    away = []
    for k, owner in enumerate(order):
        swaps[k].wait_recv()
        both = x_ref[owner * 2 + core].astype(jnp.float32) + pair[k].astype(jnp.float32)
        if k < chips - 1:
            pair[k] = both.astype(pair.dtype)
            copy = remote(pair.at[k], held.at[k], send_sem.at[k], recv_sem.at[k], targets[k])
            copy.start()
            away.append(copy)
        else:
            out_ref[...] = both
    yield
    for k, copy in enumerate(away):
        copy.wait_recv()
        out_ref[...] += held[k].astype(jnp.float32)
    for copy in away + swaps:
        copy.wait_send()
    yield


def scatter_kernel(shards, ctx, x_ref, out_ref, *scratch):
    greet(scatter_targets(shards, ctx))
    for _ in scatter_steps(shards, ctx, x_ref, out_ref, *scratch):
        pass


def scatter_scratch(blocks, chips):
    shape = blocks.shape[1:]
    return [
        pltpu.VMEM((chips,) + shape, blocks.dtype),
        pltpu.VMEM((chips - 1,) + shape, blocks.dtype),
    ] + dma_sems(chips - 1, chips - 1, chips, chips)


def both_kernel(n, shards, ctx, count, part_ref, *refs):
    blocks, total_ref, owns, scratch = (
        refs[:count],
        refs[count],
        refs[count + 1 : 2 * count + 1],
        refs[2 * count + 1 :],
    )
    me, peers = tp_peers(n)
    greet([{"tp": peer} for peer in peers] + scatter_targets(shards, ctx))
    along = tp_steps(n, part_ref, total_ref, *scratch[:5])
    across = [
        scatter_steps(shards, ctx, blocks[i], owns[i], *scratch[5 + 6 * i : 11 + 6 * i])
        for i in range(count)
    ]
    next(along)
    for steps in across:
        next(steps)
    for steps in across:
        next(steps)
    next(along)
    for steps in across:
        next(steps)
    next(along)


def sum_and_scatter(part, arrays, n, shards, ctx, collective_id):
    rows, width = part.shape
    arrays = [array.reshape(shards * ctx, -1, array.shape[1]) for array in arrays]
    scratch = [pltpu.VMEM((n - 1, rows // n, width), part.dtype)]
    scratch += dma_sems(n - 1, n - 1, n - 1, n - 1)
    for array in arrays:
        scratch += scatter_scratch(array, shards * ctx // 2)
    total, *owns = pl.pallas_call(
        functools.partial(both_kernel, n, shards, ctx, len(arrays)),
        out_shape=(jax.ShapeDtypeStruct(part.shape, part.dtype),)
        + tuple(jax.ShapeDtypeStruct(array.shape[1:], jnp.float32) for array in arrays),
        in_specs=[VMEM_SPEC] * (1 + len(arrays)),
        out_specs=(VMEM_SPEC,) * (1 + len(arrays)),
        scratch_shapes=scratch,
        compiler_params=params(collective_id),
        cost_estimate=pl.CostEstimate(flops=0, bytes_accessed=120_000_000, transcendentals=0),
        name="sum_and_scatter",
    )(part, *arrays)
    return total.astype(jnp.float32), owns


def scatter(blocks, shards, ctx, collective_id):
    count = shards * ctx
    chips = count // 2
    shape = blocks.shape[1:]
    return pl.pallas_call(
        functools.partial(scatter_kernel, shards, ctx),
        out_shape=jax.ShapeDtypeStruct(shape, jnp.float32),
        in_specs=[VMEM_SPEC],
        out_specs=VMEM_SPEC,
        scratch_shapes=scatter_scratch(blocks, chips),
        compiler_params=params(collective_id),
        cost_estimate=pl.CostEstimate(flops=0, bytes_accessed=1000, transcendentals=0),
        name="scatter_blocks",
    )(blocks)


def bounds(lengths_ref, seq, block):
    rows = lax.broadcasted_iota(jnp.int32, (block, 1), 0) + lax.axis_index("ctx") * block
    return jnp.minimum(rows, lengths_ref[seq] - 1)


def attend_kernel(groups, lengths_ref, query_ref, kv_ref, out_ref, log_ref):
    ctx, rows, both = kv_ref.shape
    width = both // 2
    block = rows // groups
    seq_len = ctx * block

    def one_sequence(seq, carry):
        span = pl.ds(pl.multiple_of(seq * block, block), block)
        columns = lax.broadcasted_iota(jnp.int32, (block, seq_len), 1)
        allowed = columns <= bounds(lengths_ref, seq, block)
        for head in range(width // HD):
            low, high = head * HD, (head + 1) * HD
            keys = kv_ref[:, span, low:high].reshape(seq_len, HD)
            values = kv_ref[:, span, width + low : width + high].reshape(seq_len, HD)
            scores = contract_last(query_ref[span, low:high], keys) * (1.0 / math.sqrt(HD))
            scores = jnp.where(allowed, scores, -1e30)
            top = jnp.max(scores, axis=1, keepdims=True)
            log_total = top + jnp.log(
                jnp.sum(jnp.where(allowed, jnp.exp(scores - top), 0.0), axis=1, keepdims=True)
            )
            probs = jnp.where(allowed, jnp.exp(scores - log_total), 0.0).astype(jnp.bfloat16)
            out_ref[span, low:high] = jnp.dot(
                probs, values, preferred_element_type=jnp.float32
            ).astype(out_ref.dtype)
            log_ref[span, head : head + 1] = log_total
        return carry

    lax.fori_loop(0, groups, one_sequence, 0)


def attend_back_kernel(
    groups, lengths_ref, query_ref, kv_ref, grad_ref, out_ref, log_ref, d_query_ref, d_kv_ref
):
    ctx, rows, both = kv_ref.shape
    width = both // 2
    block = rows // groups
    scale = 1.0 / math.sqrt(HD)

    def one_sequence(seq, carry):
        span = pl.ds(pl.multiple_of(seq * block, block), block)
        limit = bounds(lengths_ref, seq, block)
        for head in range(width // HD):
            low, high = head * HD, (head + 1) * HD
            query = query_ref[span, low:high]
            grad = grad_ref[span, low:high]
            log_total = log_ref[span, head : head + 1]
            delta = jnp.sum(
                grad.astype(jnp.float32) * out_ref[span, low:high].astype(jnp.float32),
                axis=1,
                keepdims=True,
            )
            d_query = jnp.zeros((block, HD), jnp.float32)
            for piece in range(ctx):
                keys = kv_ref[piece, span, low:high]
                values = kv_ref[piece, span, width + low : width + high]
                columns = lax.broadcasted_iota(jnp.int32, (block, block), 1) + piece * block
                scores = contract_last(query, keys) * scale
                probs = jnp.where(columns <= limit, jnp.exp(scores - log_total), 0.0)
                d_scores = (probs * (contract_last(grad, values) - delta)).astype(jnp.bfloat16)
                d_query += jnp.dot(d_scores, keys, preferred_element_type=jnp.float32)
                d_kv_ref[piece, span, low:high] = (contract_first(d_scores, query) * scale).astype(
                    d_kv_ref.dtype
                )
                d_kv_ref[piece, span, width + low : width + high] = contract_first(
                    probs.astype(jnp.bfloat16), grad
                ).astype(d_kv_ref.dtype)
            d_query_ref[span, low:high] = d_query * scale
        return carry

    lax.fori_loop(0, groups, one_sequence, 0)


def attention_call(kernel, groups, out_shape, lengths, *arrays):
    return pl.pallas_call(
        functools.partial(kernel, groups),
        out_shape=out_shape,
        in_specs=[pl.BlockSpec(memory_space=pltpu.SMEM)] + [VMEM_SPEC] * len(arrays),
        out_specs=(VMEM_SPEC,) * 2,
        compiler_params=pltpu.CompilerParams(vmem_limit_bytes=48 * 2**20),
        cost_estimate=pl.CostEstimate(flops=0, bytes_accessed=30_000_000, transcendentals=0),
        name=kernel.__name__,
    )(lengths, *arrays)


def small_kernel(shards, ctx, x_ref, out_ref, held, send_sem, recv_sem):
    count = shards * ctx
    me = lax.axis_index("shard") * ctx + lax.axis_index("ctx")
    peers = [lax.rem(me + k, count) for k in range(1, count)]
    targets = [{"shard": peer // ctx, "ctx": lax.rem(peer, ctx)} for peer in peers]
    greet(targets)
    copies = [
        remote(x_ref, held.at[k], send_sem.at[k], recv_sem.at[k], target)
        for k, target in enumerate(targets)
    ]
    for copy in copies:
        copy.start()
    out_ref[...] = x_ref[...]
    for k, copy in enumerate(copies):
        copy.wait_recv()
        out_ref[...] += held[k]
    for copy in copies:
        copy.wait_send()


def small_sum(part, shards, ctx, collective_id):
    count = shards * ctx
    return pl.pallas_call(
        functools.partial(small_kernel, shards, ctx),
        out_shape=jax.ShapeDtypeStruct(part.shape, part.dtype),
        in_specs=[VMEM_SPEC],
        out_specs=VMEM_SPEC,
        scratch_shapes=[pltpu.VMEM((count - 1,) + part.shape, part.dtype)]
        + dma_sems(count - 1, count - 1),
        compiler_params=params(collective_id),
        name="small_sum",
    )(part)


def on_device(
    shards,
    ctx,
    tp,
    hidden_in,
    lengths,
    cotangent,
    ln1_gain,
    ln1_bias,
    w_qkv,
    b_qv,
    w_out,
    b_out,
    ln2_gain,
    ln2_bias,
    w_up,
    b_up,
    w_down,
    b_down,
):
    groups, block_len, width = hidden_in.shape
    head_width = w_qkv.shape[2]
    heads_here = head_width // HD
    row_count = groups * block_len
    rows_own = w_out.shape[0]
    vectors = jnp.stack([ln1_gain, ln1_bias, b_out, ln2_gain, ln2_bias, b_down], 1)
    packed_one = jnp.concatenate(
        [w_qkv[0], w_qkv[1], w_qkv[2], w_out, jnp.pad(vectors, ((0, 0), (0, 122)))], 1
    )
    out_rows = lax.all_gather(w_out, "tp", axis=1, tiled=True)
    packed_two = jnp.concatenate([w_up, w_down, out_rows], 1)
    whole_one = gather(packed_one, shards, ctx, 2).reshape(-1, packed_one.shape[1])
    packed_two, whole_one = lax.optimization_barrier((packed_two, whole_one))
    whole_two = lax.all_gather(packed_two, ("shard", "ctx"), axis=0, tiled=True)
    qkv_width = 3 * head_width
    qkv_full = whole_one[:, :qkv_width]
    out_full = whole_one[:, qkv_width : qkv_width + head_width]
    vec_wide = whole_one[:, qkv_width + head_width :].astype(jnp.float32).T
    up_full = whole_two[:, : w_up.shape[1]]
    down_full = whole_two[:, w_up.shape[1] : 2 * w_up.shape[1]]
    out_wide = whole_two[:, 2 * w_up.shape[1] :]
    gain_one = vec_wide[0]
    shift_one = vec_wide[1]
    bias_out = vec_wide[2]
    gain_two = vec_wide[3]
    shift_two = vec_wide[4]
    bias_down = vec_wide[5]
    ctx_index = lax.axis_index("ctx")
    positions = jnp.arange(block_len, dtype=jnp.int32) + ctx_index * block_len
    live_rows = (positions[None, :] < lengths[:, None]).reshape(row_count, 1)

    inputs = hidden_in.reshape(row_count, width).astype(jnp.float32)
    normed_one, unit_one, inv_one = normalize(inputs, gain_one, shift_one)
    normed_bf = normed_one.astype(jnp.bfloat16)
    product = jnp.dot(normed_bf, qkv_full, preferred_element_type=jnp.float32)
    projected = [product[:, j * head_width : (j + 1) * head_width] for j in range(3)]
    query = (projected[0] + b_qv[0].astype(jnp.float32)).astype(jnp.bfloat16)
    keys_here = projected[1].astype(jnp.bfloat16).reshape(groups, block_len, head_width)
    values_here = (
        (projected[2] + b_qv[1].astype(jnp.float32))
        .astype(jnp.bfloat16)
        .reshape(groups, block_len, head_width)
    )
    kv_blocks = gather(
        jnp.concatenate([keys_here, values_here], -1).reshape(row_count, 2 * head_width), 1, ctx, 3
    )
    attended, log_total = attention_call(
        attend_kernel,
        groups,
        (
            jax.ShapeDtypeStruct(query.shape, jnp.bfloat16),
            jax.ShapeDtypeStruct((row_count, heads_here), jnp.float32),
        ),
        lengths,
        query,
        kv_blocks,
    )
    proj_sum = contract_last(gather_tp(attended, tp), out_wide)
    resid = inputs + proj_sum + bias_out
    normed_two, unit_two, inv_two = normalize(resid, gain_two, shift_two)
    second_bf = normed_two.astype(jnp.bfloat16)
    pre_act = jnp.dot(second_bf, up_full, preferred_element_type=jnp.float32) + b_up.astype(
        jnp.float32
    )
    activ, slope = gelu_pair(pre_act)
    hidden = activ.astype(jnp.bfloat16)
    grad_rows = jnp.where(live_rows, cotangent.reshape(row_count, width).astype(jnp.float32), 0.0)
    grad_bf = grad_rows.astype(jnp.bfloat16)
    grad_bias_down = jnp.sum(grad_rows, axis=0)
    grad_down = contract_first(grad_bf, hidden)
    d_pre = jnp.dot(grad_bf, down_full, preferred_element_type=jnp.float32) * slope
    d_pre_bf = d_pre.astype(jnp.bfloat16)
    grad_bias_up = jnp.sum(d_pre, axis=0)
    grad_up = contract_first(second_bf, d_pre_bf)
    back_part = contract_last(d_pre_bf, up_full).astype(jnp.bfloat16)
    back_two, (sum_up, sum_down) = sum_and_scatter(
        back_part,
        [grad_up.astype(jnp.bfloat16), grad_down.astype(jnp.bfloat16)],
        tp,
        shards,
        ctx,
        1,
    )
    mlp_part = contract_last(hidden, down_full).astype(jnp.bfloat16)
    mlp_part, back_two = lax.optimization_barrier((mlp_part, back_two))
    mlp_sum = lax.psum(mlp_part, "tp")
    grad_gain_two = jnp.sum(back_two * unit_two, axis=0)
    grad_shift_two = jnp.sum(back_two, axis=0)
    d_resid = grad_rows + normalize_back(back_two, unit_two, inv_two, gain_two)
    d_resid_bf = d_resid.astype(jnp.bfloat16)
    grad_bias_out = jnp.sum(d_resid, axis=0)
    grad_out = contract_first(d_resid_bf, attended)
    d_attended = jnp.dot(d_resid_bf, out_full, preferred_element_type=jnp.float32).astype(
        jnp.bfloat16
    )
    d_query_rows, kv_blocks_grad = attention_call(
        attend_back_kernel,
        groups,
        (
            jax.ShapeDtypeStruct(query.shape, jnp.float32),
            jax.ShapeDtypeStruct(kv_blocks.shape, jnp.bfloat16),
        ),
        lengths,
        query,
        kv_blocks,
        d_attended,
        attended,
        log_total,
    )
    kv_sum = scatter(kv_blocks_grad, 1, ctx, 4)
    d_keys, d_values = kv_sum[..., :head_width], kv_sum[..., head_width:]
    d_value_rows = d_values.reshape(row_count, head_width)
    grad_bias_qv = jnp.stack([jnp.sum(d_query_rows, axis=0), jnp.sum(d_value_rows, axis=0)], 0)
    stacked = jnp.concatenate(
        [d_query_rows, d_keys, d_value_rows], 1
    ).astype(jnp.bfloat16)
    grad_qkv = contract_first(normed_bf, stacked)
    first_part = contract_last(stacked, qkv_full).astype(jnp.bfloat16)
    mlp_sum, first_part = lax.optimization_barrier((mlp_sum, first_part))
    result = jnp.where(live_rows, resid + mlp_sum.astype(jnp.float32) + bias_down, 0.0)
    back_one, (sum_back, sum_out) = sum_and_scatter(
        first_part,
        [grad_qkv.astype(jnp.bfloat16), grad_out.astype(jnp.bfloat16)],
        tp,
        shards,
        ctx,
        6,
    )
    grad_gain_one = jnp.sum(back_one * unit_one, axis=0)
    grad_shift_one = jnp.sum(back_one, axis=0)
    d_inputs = d_resid + normalize_back(back_one, unit_one, inv_one, gain_one)
    vec_grads = jnp.concatenate(
        [
            grad_gain_one,
            grad_shift_one,
            grad_bias_out,
            grad_gain_two,
            grad_shift_two,
            grad_bias_down,
            grad_bias_qv.reshape(-1),
            grad_bias_up,
        ]
    )
    sum_qkv = jnp.stack(
        [sum_back[:, j * head_width : (j + 1) * head_width] for j in range(3)], 0
    )
    all_vec = small_sum(vec_grads.reshape(-1, 128), shards, ctx, 5).reshape(-1)
    own = lax.axis_index(("shard", "ctx")) * rows_own
    sum_vec = lax.dynamic_slice(all_vec[: 6 * width].reshape(6, width), (0, own), (6, rows_own))
    bias_qv_sum = all_vec[6 * width : 6 * width + 2 * head_width].reshape(2, head_width)
    bias_up_sum = all_vec[6 * width + 2 * head_width :]
    return (
        result.reshape(groups, block_len, width),
        d_inputs.reshape(groups, block_len, width),
        sum_vec[0],
        sum_vec[1],
        sum_qkv,
        bias_qv_sum,
        sum_out,
        sum_vec[2],
        sum_vec[3],
        sum_vec[4],
        sum_up,
        bias_up_sum,
        sum_down,
        sum_vec[5],
    )


def solution(mesh):
    return jax.shard_map(
        functools.partial(
            on_device, mesh.shape["shard"], mesh.shape["ctx"], mesh.shape["tp"]
        ),
        mesh=mesh,
        in_specs=(
            P("shard", "ctx", None),
            P("shard"),
            P("shard", "ctx", None),
            P(("shard", "ctx")),
            P(("shard", "ctx")),
            P(None, ("shard", "ctx"), "tp"),
            P(None, "tp"),
            P(("shard", "ctx"), "tp"),
            P(("shard", "ctx")),
            P(("shard", "ctx")),
            P(("shard", "ctx")),
            P(("shard", "ctx"), "tp"),
            P("tp"),
            P(("shard", "ctx"), "tp"),
            P(("shard", "ctx")),
        ),
        out_specs=(
            P("shard", "ctx", None),
            P("shard", "ctx", None),
            P(("shard", "ctx")),
            P(("shard", "ctx")),
            P(None, ("shard", "ctx"), "tp"),
            P(None, "tp"),
            P(("shard", "ctx"), "tp"),
            P(("shard", "ctx")),
            P(("shard", "ctx")),
            P(("shard", "ctx")),
            P(("shard", "ctx"), "tp"),
            P("tp"),
            P(("shard", "ctx"), "tp"),
            P(("shard", "ctx")),
        ),
        check_vma=False,
    )
```
